512 devices in a mesh: dp: 4 (over y_hi), ctx: 32 (over z, y_lo, core), head: 4 (over x).
Axes of the slice: x: 4, y: 8 (y_hi: 4, y_lo: 2; y = y_hi * 2 + y_lo), z: 8, core: 2. Of those that a mesh axis runs over, the one named last changes fastest.
Arguments:
- enc_query: bfloat16 [32768, 4096], P(('dp', 'ctx'), 'head'), parts along dimension 0, may hold values from -30 to 30
- enc_key: bfloat16 [32768, 4096], P(('dp', 'ctx'), 'head'), parts along dimension 0, may hold values from -6 to 6
- enc_value: bfloat16 [32768, 4096], P(('dp', 'ctx'), 'head'), parts along dimension 0, may hold values from -6 to 6
- doc_ids: int32 [32768], P(('dp', 'ctx')), parts along dimension 0, may hold values from 0 to 95, never falling along the last dimension, each value on 1 to 256 neighbouring positions
- key_map: bfloat16 [4096, 2048], P('ctx', 'head'), may hold values from -0.09375 to 0.09375
- value_map: bfloat16 [4096, 2048], P('ctx', 'head'), may hold values from -0.09375 to 0.09375
- tgt_query: bfloat16 [8192, 2048], P(('dp', 'ctx'), 'head'), parts along dimension 0, may hold values from -150 to 150
Outputs:
- cross_out: bfloat16 [8192, 2048], P(('dp', 'ctx'), 'head'), parts along dimension 0
The draws below stay inside these ranges and needn't reach their ends.
There are 4 independent parts, one for each index of `dp`. The reference program is written for one: setup_inputs(seed, part) draws one part's arguments, and reference() takes and returns one part's arrays. A program takes and returns all parts, laid end to end along the dimension named above; an argument that names none is the same for every part. Nothing has to cross between parts.
Inputs may be any that keep to these rules, and one draw needn't show every extreme that they name: `doc_ids`: document ids never fall along the pack; each document holds 1 to 256 consecutive positions and one holds exactly 256.
All inputs are finite; a program needn't handle non-finite values.
Results may differ from the reference program's by a relative error of at most 0.011.
Values may be sent and summed in bfloat16 or wider, within the bound.
A program may use at most 64 MiB of HBM per device.

```python
import math
import jax
import jax.numpy as jnp
import numpy as np
from jax import lax

HEADS = 16
HEAD_DIM = 256
CROSS_HEADS = 8
TOK_DEV = 256
TGT_DEV = 64
S_IN = 8192
S_TG = 2048
DOCS = 96
N_CTX = 32


def key_rows(key):
    shape = (S_IN, HEADS * HEAD_DIM)
    return jnp.clip(jax.random.normal(jax.random.fold_in(key, 7), shape, jnp.float32), -6.0, 6.0)


def draw_enc_key(key, part):
    return key_rows(key).astype(jnp.bfloat16)


def draw_enc_query(key, part):
    shape = (S_IN, HEADS * HEAD_DIM)
    fresh = jnp.clip(jax.random.normal(jax.random.fold_in(key, 8), shape, jnp.float32), -6.0, 6.0)
    return fresh.astype(jnp.bfloat16)


def draw_tgt_query(key, part):
    shape = (S_TG, CROSS_HEADS * HEAD_DIM)
    fresh = jnp.clip(jax.random.normal(jax.random.fold_in(key, 11), shape, jnp.float32), -6.0, 6.0)
    return fresh.astype(jnp.bfloat16)


def levels(key, extent, pieces, least, top_value):
    factor_of = 1.0
    for position, blocks in pieces:
        heights = jax.random.uniform(jax.random.fold_in(jax.random.fold_in(key, 6), position), (blocks,), jnp.float32, least / len(pieces), top_value / len(pieces))
        factor_of = factor_of * jnp.repeat(jnp.exp(heights), extent[position] // blocks).reshape((-1,) + (1,) * (len(extent) - 1 - position))
    return factor_of


def length_profile(amount, total, most, skew):
    loads = [(1 << 20) // math.isqrt(grade ** skew) + 1 for grade in range(2, amount + 1)]
    surplus, given = total - most - (amount - 1), [1] * (amount - 1)
    while surplus > 0:
        movable = [i for i in range(amount - 1) if given[i] < most]
        mass, left = sum([loads[i] for i in movable]), surplus
        for i in movable:
            extra = min(most - given[i], max(1, left * loads[i] // mass), surplus)
            given[i] = given[i] + extra
            surplus = surplus - extra
    return np.array([most] + given)


def uneven(stream_key, count, total, limit, lean):
    if count == 2:
        one = jax.random.randint(stream_key, (), max(1, total - limit), min(limit, total - 1) + 1)
        return jnp.stack([one, total - one])
    lengths = jnp.asarray(length_profile(count, total, limit, lean), jnp.int32)
    couples = (count - 1) // 2
    source_of, receiver = lengths[1:1 + 2 * couples:2], lengths[2:2 + 2 * couples:2]
    margin = jnp.minimum(source_of - 1, limit - receiver)
    shifted = jax.random.randint(jax.random.fold_in(stream_key, 1), (couples,), 0, 1 << 20) % (margin + 1)
    lengths = lengths.at[1:1 + 2 * couples:2].set(source_of - shifted).at[2:2 + 2 * couples:2].set(receiver + shifted)
    return lengths[jax.random.permutation(jax.random.fold_in(stream_key, 2), count)]


def centred(stream_key, shape, spread, most, shards=(), kind=jnp.bfloat16):
    level = levels(stream_key, shape, shards, -0.22, 0.18) if shards else 1.0
    result = jax.random.normal(stream_key, shape, jnp.float32) * spread * level
    return jnp.minimum(jnp.maximum(result, -most), most).astype(kind)


def setup_inputs(seed: int = 0, part: int = 0) -> dict:
    seeds = jax.random.split(jax.random.key(seed), 8)
    own_keys = jax.random.split(jax.random.fold_in(seeds[7], part), 8)
    return {
        "enc_query": draw_enc_query(jax.random.fold_in(jax.random.fold_in(seeds[7], part), 71), part),
        "enc_key": draw_enc_key(jax.random.fold_in(jax.random.fold_in(seeds[7], part), 71), part),
        "enc_value": centred(own_keys[2], (S_IN, HEADS * HEAD_DIM), 1.0, 6.0, ((0, 32), (1, 4))),
        "doc_ids": jnp.searchsorted(jnp.cumsum(uneven(own_keys[3], DOCS, S_IN, TOK_DEV, 2)), jnp.arange(S_IN), side="right").astype(jnp.int32),
        "key_map": centred(seeds[4], (HEADS * HEAD_DIM, CROSS_HEADS * HEAD_DIM), (HEADS * HEAD_DIM) ** -0.5, 0.09375, ((0, 32), (1, 4))),
        "value_map": centred(seeds[5], (HEADS * HEAD_DIM, CROSS_HEADS * HEAD_DIM), (HEADS * HEAD_DIM) ** -0.5, 0.09375, ((0, 32), (1, 4))),
        "tgt_query": draw_tgt_query(jax.random.fold_in(jax.random.fold_in(seeds[7], part), 71), part),
    }


NEG_FILL = -1e30


def attend(query, keys, values, query_mark, key_mark):
    scale = HEAD_DIM ** -0.5
    scores = jnp.einsum("rhe,khe->hrk", query.astype(jnp.float32), keys.astype(jnp.float32), precision=lax.Precision.HIGHEST) * scale
    same = query_mark[:, None] == key_mark[None, :]
    scores = jnp.where(same[None], scores, NEG_FILL)
    top = jnp.max(scores, axis=2, keepdims=True)
    weights = jnp.exp(scores - top)
    total = jnp.sum(weights, axis=2)
    rounded = lax.optimization_barrier(weights.astype(jnp.bfloat16)).astype(jnp.float32)
    summed = jnp.einsum("hrk,khe->rhe", rounded, values.astype(jnp.float32), precision=lax.Precision.HIGHEST)
    return summed / jnp.transpose(total)[:, :, None]


def padded_rows(array, fill_value):
    edge = jnp.full((TOK_DEV,) + array.shape[1:], fill_value, array.dtype)
    return jnp.concatenate([edge, array, edge], 0)


def reference(enc_query, enc_key, enc_value, doc_ids, key_map, value_map, tgt_query):
    blocks = N_CTX
    query = enc_query.reshape(blocks, TOK_DEV, HEADS, HEAD_DIM)
    keys = padded_rows(enc_key.reshape(S_IN, HEADS, HEAD_DIM), 0.0)
    values = padded_rows(enc_value.reshape(S_IN, HEADS, HEAD_DIM), 0.0)
    marks = padded_rows(doc_ids, -1)
    query_marks = doc_ids.reshape(blocks, TOK_DEV)

    def encoder_block(index):
        start = (index * TOK_DEV).astype(jnp.int32)
        window_keys = lax.dynamic_slice_in_dim(keys, start, 3 * TOK_DEV, 0)
        window_values = lax.dynamic_slice_in_dim(values, start, 3 * TOK_DEV, 0)
        window_marks = lax.dynamic_slice_in_dim(marks, start, 3 * TOK_DEV, 0)
        return attend(query[index], window_keys, window_values, query_marks[index], window_marks).astype(jnp.bfloat16)

    enc_out = lax.map(encoder_block, jnp.arange(blocks, dtype=jnp.int32)).reshape(S_IN, HEADS * HEAD_DIM)
    memory_key = jnp.dot(enc_out, key_map, preferred_element_type=jnp.float32).astype(jnp.bfloat16)
    memory_value = jnp.dot(enc_out, value_map, preferred_element_type=jnp.float32).astype(jnp.bfloat16)
    memory_keys = padded_rows(memory_key.reshape(S_IN, CROSS_HEADS, HEAD_DIM), 0.0)
    memory_values = padded_rows(memory_value.reshape(S_IN, CROSS_HEADS, HEAD_DIM), 0.0)
    target_doc = doc_ids.reshape(S_TG, 4)[:, 0]
    target_marks = target_doc.reshape(blocks, TGT_DEV)
    target = tgt_query.reshape(blocks, TGT_DEV, CROSS_HEADS, HEAD_DIM)

    def cross_block(index):
        start = (index * TOK_DEV).astype(jnp.int32)
        window_keys = lax.dynamic_slice_in_dim(memory_keys, start, 3 * TOK_DEV, 0)
        window_values = lax.dynamic_slice_in_dim(memory_values, start, 3 * TOK_DEV, 0)
        window_marks = lax.dynamic_slice_in_dim(marks, start, 3 * TOK_DEV, 0)
        return attend(target[index], window_keys, window_values, target_marks[index], window_marks).astype(jnp.bfloat16)

    cross_out = lax.map(cross_block, jnp.arange(blocks, dtype=jnp.int32))
    return cross_out.reshape(S_TG, CROSS_HEADS * HEAD_DIM)
```

```python
import functools

import jax
import jax.numpy as jnp
from jax import lax
from jax.experimental import pallas as pl
from jax.experimental.pallas import tpu as pltpu
from jax.sharding import PartitionSpec as P

MESH = pl.DeviceIdType.MESH
HEAD_DIM = 256
NEG_FILL = -1e30
SCALE = HEAD_DIM ** (-0.5)
F32 = jnp.float32
BF16 = jnp.bfloat16


def nt(a, b):
    return lax.dot_general(a, b, (((1,), (1,)), ((), ())), preferred_element_type=F32)


def nn(a, b):
    return lax.dot_general(a, b, (((1,), (0,)), ((), ())), preferred_element_type=F32)


def column_of(row, count, step):
    n = row.shape[1]
    i = lax.broadcasted_iota(jnp.int32, (count, n), 0)
    j = lax.broadcasted_iota(jnp.int32, (count, n), 1)
    return jnp.sum(jnp.where(j == step * i, row, 0.0), axis=1, keepdims=True)


def kernel(
    sizes,
    q_hbm,
    k_hbm,
    v_hbm,
    docs_hbm,
    wk_hbm,
    wv_hbm,
    tq_hbm,
    out_ref,
    qv,
    kb,
    vb,
    docs,
    tq,
    wk,
    wv,
    enc,
    mem,
    part_out,
    part_in,
    local_sem,
    halo_s,
    halo_r,
    small_s,
    small_r,
    zs,
    zr,
    ys,
    yr,
    ss,
    sr,
    xs,
    xr,
    xfs,
    xfr,
    cs,
    cr,
):
    n_dp, n_ctx, n_x = sizes
    n_z = n_ctx // 4
    dp = lax.axis_index("dp")
    ctx = lax.axis_index("ctx")
    x = lax.axis_index("head")
    core = lax.rem(ctx, 2)
    yl = lax.rem(ctx // 2, 2)
    z = ctx // 4

    heads = k_hbm.shape[1] // HEAD_DIM
    rows = k_hbm.shape[0]
    tgts = tq_hbm.shape[0]
    crosses = wk_hbm.shape[1] // HEAD_DIM
    wrows = wk_hbm.shape[0]

    left = (dp, lax.rem(ctx + n_ctx - 1, n_ctx), x)
    right = (dp, lax.rem(ctx + 1, n_ctx), x)
    zp = (dp, lax.rem(ctx + 4, n_ctx), x)
    zm = (dp, lax.rem(ctx + n_ctx - 4, n_ctx), x)
    pair = (dp, ctx + 2 - 4 * yl, x)
    across = (lax.rem(dp + 2 * yl - 1 + n_dp, n_dp), ctx + 2 - 4 * yl, x)
    sib = (dp, ctx + 1 - 2 * core, x)
    xp = (dp, ctx, lax.rem(x + 1, n_x))
    xm = (dp, ctx, lax.rem(x + n_x - 1, n_x))

    def remote(src, dst, send, recv, device):
        return pltpu.make_async_remote_copy(
            src_ref=src, dst_ref=dst, send_sem=send, recv_sem=recv,
            device_id=device, device_id_type=MESH,
        )

    barrier = pltpu.get_barrier_semaphore()
    partners = (left, right, zp, zm, pair, across, sib, xp, xm)
    for device in partners:
        pl.semaphore_signal(barrier, inc=1, device_id=device, device_id_type=MESH)

    locals_ = [
        pltpu.make_async_copy(docs_hbm, docs.at[1], local_sem.at[0]),
        pltpu.make_async_copy(q_hbm, qv, local_sem.at[1]),
        pltpu.make_async_copy(tq_hbm, tq.at[1], local_sem.at[2]),
    ]
    for h in range(heads):
        cols = pl.ds(h * HEAD_DIM, HEAD_DIM)
        locals_.append(pltpu.make_async_copy(k_hbm.at[:, cols], kb.at[1, h], local_sem.at[3 + 2 * h]))
        locals_.append(pltpu.make_async_copy(v_hbm.at[:, cols], vb.at[1, h], local_sem.at[4 + 2 * h]))

    def shard(zz, yy, cc):
        return pl.ds(pl.multiple_of((zz * 4 + yy * 2 + cc) * wrows, wrows), wrows)

    own_rows = shard(z, yl, core)
    base = 3 + 2 * heads
    locals_.append(pltpu.make_async_copy(wk_hbm, wk.at[own_rows], local_sem.at[base]))
    locals_.append(pltpu.make_async_copy(wv_hbm, wv.at[own_rows], local_sem.at[base + 1]))
    for copy in locals_:
        copy.start()

    pl.semaphore_wait(barrier, len(partners))

    sends = []

    def go(copy):
        copy.start()
        sends.append(copy)
        return copy

    sides = ((left, 2), (right, 0))
    halo = {}
    small = {}
    for side, (device, slot) in enumerate(sides):
        small[side, 0] = go(remote(docs_hbm, docs.at[slot], small_s.at[side, 0], small_r.at[side, 0], device))

    def start_halo(h):
        cols = pl.ds(h * HEAD_DIM, HEAD_DIM)
        for side, (device, slot) in enumerate(sides):
            halo[side, 0, h] = go(remote(
                k_hbm.at[:, cols], kb.at[slot, h], halo_s.at[side, 0, h], halo_r.at[side, 0, h], device))
            halo[side, 1, h] = go(remote(
                v_hbm.at[:, cols], vb.at[slot, h], halo_s.at[side, 1, h], halo_r.at[side, 1, h], device))

    w_of = (wk, wv)
    w_hbm = (wk_hbm, wv_hbm)
    zmove, ymove, smove = {}, {}, {}

    def zz_of(d):
        return lax.rem(z + d + n_z, n_z)

    def send_z(direction, step, kv, src):
        d = (1 - step) if direction == 0 else (step - 1)
        at = shard(zz_of(d), yl, core)
        device = zp if direction == 0 else zm
        if src is None:
            src = w_of[kv].at[at]
        zmove[direction, step, kv] = go(remote(
            src, w_of[kv].at[at], zs.at[direction, step - 1, kv], zr.at[direction, step - 1, kv], device))

    def send_y(d, kv, src):
        at = shard(zz_of(d), yl, core)
        far = (abs(d) == 3 and kv == 0) or abs(d) == 4
        device = pair if far else across
        if src is None:
            src = w_of[kv].at[at]
        ymove[d, kv] = go(remote(
            src, w_of[kv].at[at], ys.at[d + 3, kv], yr.at[d + 3, kv], device))

    def send_sib(parity, d, kv, src):
        yy = yl if parity == 0 else 1 - yl
        at = shard(zz_of(d), yy, core)
        if src is None:
            src = w_of[kv].at[at]
        smove[parity, d, kv] = go(remote(
            src, w_of[kv].at[at], ss.at[parity, d + 3, kv], sr.at[parity, d + 3, kv], sib))

    half = n_z // 2

    def arrive_z(direction, step, kv):
        zmove[direction, step, kv].wait_recv()
        d = -step if direction == 0 else step
        if step == half:
            d = half
        if step + 1 < half or (step + 1 == half and kv == direction):
            send_z(direction, step + 1, kv, None)
        send_y(d, kv, None)
        send_sib(0, d, kv, None)

    def arrive_y(d, kv):
        ymove[d, kv].wait_recv()
        send_sib(1, d, kv, None)

    def ring_step(step):
        for kv in range(2):
            for direction in range(2):
                if step < half or kv == direction:
                    arrive_z(direction, step, kv)

    start_halo(0)
    for kv in range(2):
        send_z(0, 1, kv, w_hbm[kv])
        send_z(1, 1, kv, w_hbm[kv])
        send_y(0, kv, w_hbm[kv])
    for h in range(1, heads):
        start_halo(h)
    for kv in range(2):
        send_sib(0, 0, kv, w_hbm[kv])
    for side, (device, slot) in enumerate(sides):
        small[side, 1] = go(remote(tq_hbm, tq.at[slot], small_s.at[side, 1], small_r.at[side, 1], device))

    for copy in locals_:
        copy.wait()
    for side in range(2):
        small[side, 0].wait_recv()

    marks = [docs[slot, 0:1, :] for slot in range(3)]
    own_col = column_of(marks[1], rows, 1)

    xmove, xfwd = {}, {}

    def attend(h):
        for side in range(2):
            for kv in range(2):
                halo[side, kv, h].wait_recv()
        query = qv[:, h * HEAD_DIM:(h + 1) * HEAD_DIM]
        scores = []
        for slot in range(3):
            raw = nt(query, kb[slot, h]) * SCALE
            scores.append(jnp.where(own_col == marks[slot], raw, NEG_FILL))
        top = jnp.max(jnp.maximum(jnp.maximum(scores[0], scores[1]), scores[2]), axis=1, keepdims=True)
        weights = [jnp.exp(s - top) for s in scores]
        total = jnp.sum(weights[0] + weights[1] + weights[2], axis=1, keepdims=True)
        summed = sum(nn(weights[slot].astype(BF16), vb[slot, h]) for slot in range(3))
        at = pl.ds(pl.multiple_of((x * heads + h) * HEAD_DIM, HEAD_DIM), HEAD_DIM)
        enc[:, at] = (summed / total).astype(BF16)
        for side, device in enumerate((xp, xm)):
            xmove[side, h] = go(remote(enc.at[:, at], enc.at[:, at], xs.at[side, h], xr.at[side, h], device))

    def hand_on(h):
        for side in range(2):
            xmove[side, h].wait_recv()
        side = h % 2
        source = lax.rem(x + n_x - 1, n_x) if side == 0 else lax.rem(x + 1, n_x)
        at = pl.ds(pl.multiple_of((source * heads + h) * HEAD_DIM, HEAD_DIM), HEAD_DIM)
        xfwd[h] = go(remote(enc.at[:, at], enc.at[:, at], xfs.at[h], xfr.at[h], (xp, xm)[side]))

    def come_y(*pieces):
        for d, kv in pieces:
            arrive_y(d, kv)

    ring_step(1)
    attend(0)
    come_y((0, 0), (0, 1))
    ring_step(2)
    hand_on(0)
    attend(1)
    come_y((-1, 0), (1, 0))
    ring_step(3)
    hand_on(1)
    attend(2)
    come_y((-1, 1), (1, 1))
    ring_step(4)
    hand_on(2)
    attend(3)
    come_y((-2, 0), (2, 0), (-2, 1), (2, 1))
    hand_on(3)
    come_y((-3, 1), (3, 1), (-3, 0), (3, 0), (4, 0), (4, 1))

    for h in range(heads):
        xfwd[h].wait_recv()
    for key in smove:
        smove[key].wait_recv()

    for kv in range(2):
        for n in range(crosses):
            cols = slice(n * HEAD_DIM, (n + 1) * HEAD_DIM)
            mem[kv, n] = nn(enc[...], w_of[kv][:, cols]).astype(BF16)

    for side in range(2):
        small[side, 1].wait_recv()
    lane = lax.broadcasted_iota(jnp.int32, (tgts, 128), 1)
    cmove = {}
    own = {}
    for n in range(crosses):
        cols = slice(n * HEAD_DIM, (n + 1) * HEAD_DIM)
        for slot in (0, 2, 1):
            col = column_of(marks[slot], tgts, rows // tgts)
            raw = nt(tq[slot, :, cols], mem[0, n]) * SCALE
            scores = jnp.where(col == marks[1], raw, NEG_FILL)
            top = jnp.max(scores, axis=1, keepdims=True)
            weights = jnp.exp(scores - top)
            total = jnp.sum(weights, axis=1, keepdims=True)
            summed = nn(weights.astype(BF16), mem[1, n])
            if slot == 1:
                own[n] = (top, total, summed)
                continue
            side = 0 if slot == 0 else 1
            part_out[side, n, :, 0:HEAD_DIM] = summed
            part_out[side, n, :, HEAD_DIM:] = jnp.where(lane == 0, top, total)
            cmove[side, n] = go(remote(
                part_out.at[side, n], part_in.at[1 - side, n], cs.at[side, n], cr.at[side, n], sides[side][0]))

    for n in range(crosses):
        top, total, summed = own[n]
        tops, totals, sums = [top], [total], [summed]
        for side in range(2):
            cmove[side, n].wait_recv()
            tops.append(part_in[1 - side, n, :, HEAD_DIM:HEAD_DIM + 1])
            totals.append(part_in[1 - side, n, :, HEAD_DIM + 1:HEAD_DIM + 2])
            sums.append(part_in[1 - side, n, :, 0:HEAD_DIM])
        most = jnp.maximum(jnp.maximum(tops[0], tops[1]), tops[2])
        factor = [jnp.exp(t - most) for t in tops]
        total = sum(f * t for f, t in zip(factor, totals))
        summed = sum(f * s for f, s in zip(factor, sums))
        out_ref[:, n * HEAD_DIM:(n + 1) * HEAD_DIM] = (summed / total).astype(BF16)

    for copy in sends:
        copy.wait_send()


def on_device(sizes, enc_query, enc_key, enc_value, doc_ids, key_map, value_map, tgt_query):
    rows, width = enc_key.shape
    heads = width // HEAD_DIM
    wrows, wcols = key_map.shape
    crosses = wcols // HEAD_DIM
    tgts = tgt_query.shape[0]
    n_z = sizes[1] // 4
    docs = jnp.broadcast_to(doc_ids.astype(F32)[None, :], (8, rows))
    dma = pltpu.SemaphoreType.DMA
    any_spec = pl.BlockSpec(memory_space=pl.ANY)
    return pl.pallas_call(
        functools.partial(kernel, sizes),
        out_shape=jax.ShapeDtypeStruct((tgts, wcols), BF16),
        in_specs=[any_spec] * 7,
        out_specs=pl.BlockSpec(memory_space=pltpu.VMEM),
        scratch_shapes=[
            pltpu.VMEM((rows, width), BF16),
            pltpu.VMEM((3, heads, rows, HEAD_DIM), BF16),
            pltpu.VMEM((3, heads, rows, HEAD_DIM), BF16),
            pltpu.VMEM((3, 8, rows), F32),
            pltpu.VMEM((3, tgts, wcols), BF16),
            pltpu.VMEM((wrows * sizes[1], wcols), BF16),
            pltpu.VMEM((wrows * sizes[1], wcols), BF16),
            pltpu.VMEM((rows, width * sizes[2]), BF16),
            pltpu.VMEM((2, crosses, rows, HEAD_DIM), BF16),
            pltpu.VMEM((2, crosses, tgts, HEAD_DIM + 128), F32),
            pltpu.VMEM((2, crosses, tgts, HEAD_DIM + 128), F32),
            dma((5 + 2 * heads,)),
            dma((2, 2, heads)),
            dma((2, 2, heads)),
            dma((2, 2)),
            dma((2, 2)),
            dma((2, n_z // 2, 2)),
            dma((2, n_z // 2, 2)),
            dma((n_z, 2)),
            dma((n_z, 2)),
            dma((2, n_z, 2)),
            dma((2, n_z, 2)),
            dma((2, heads)),
            dma((2, heads)),
            dma((heads,)),
            dma((heads,)),
            dma((2, crosses)),
            dma((2, crosses)),
        ],
        compiler_params=pltpu.CompilerParams(
            collective_id=0, has_side_effects=True, vmem_limit_bytes=60 * 1024 * 1024
        ),
    )(enc_query, enc_key, enc_value, docs, key_map, value_map, tgt_query)


def solution(mesh):
    sizes = (mesh.shape["dp"], mesh.shape["ctx"], mesh.shape["head"])
    in_specs = (
        P(("dp", "ctx"), "head"),
        P(("dp", "ctx"), "head"),
        P(("dp", "ctx"), "head"),
        P(("dp", "ctx")),
        P("ctx", "head"),
        P("ctx", "head"),
        P(("dp", "ctx"), "head"),
    )
    return jax.shard_map(
        functools.partial(on_device, sizes),
        mesh=mesh,
        in_specs=in_specs,
        out_specs=P(("dp", "ctx"), "head"),
        check_vma=False,
    )
```

```python
import functools

import jax
import jax.numpy as jnp
from jax import lax
from jax.experimental import pallas as pl
from jax.experimental.pallas import tpu as pltpu
from jax.sharding import PartitionSpec as P

MESH = pl.DeviceIdType.MESH
HEAD_DIM = 256
NEG_FILL = -1e30
SCALE = HEAD_DIM ** (-0.5)
F32 = jnp.float32
BF16 = jnp.bfloat16


def nt(a, b):
    return lax.dot_general(a, b, (((1,), (1,)), ((), ())), preferred_element_type=F32)


def nn(a, b):
    return lax.dot_general(a, b, (((1,), (0,)), ((), ())), preferred_element_type=F32)


def column_of(row, count, step):
    n = row.shape[1]
    i = lax.broadcasted_iota(jnp.int32, (count, n), 0)
    j = lax.broadcasted_iota(jnp.int32, (count, n), 1)
    return jnp.sum(jnp.where(j == step * i, row, 0.0), axis=1, keepdims=True)


def kernel(
    sizes,
    q_hbm,
    k_hbm,
    v_hbm,
    docs_hbm,
    wk_hbm,
    wv_hbm,
    tq_hbm,
    out_ref,
    qv,
    kb,
    vb,
    docs,
    tq,
    w,
    enc,
    part_out,
    part_in,
    local_sem,
    own_w_sem,
    halo_s,
    halo_r,
    small_s,
    small_r,
    zs,
    zr,
    ys,
    yr,
    ss,
    sr,
    xs,
    xr,
    xfs,
    xfr,
    cs,
    cr,
):
    n_dp, n_ctx, n_x = sizes
    n_z = n_ctx // 4
    dp = lax.axis_index("dp")
    ctx = lax.axis_index("ctx")
    x = lax.axis_index("head")
    core = lax.rem(ctx, 2)
    yl = lax.rem(ctx // 2, 2)
    z = ctx // 4
    sign = 1 - 2 * yl

    heads = k_hbm.shape[1] // HEAD_DIM
    rows = k_hbm.shape[0]
    tgts = tq_hbm.shape[0]
    crosses = wk_hbm.shape[1] // HEAD_DIM
    wrows = wk_hbm.shape[0]

    left = (dp, lax.rem(ctx + n_ctx - 1, n_ctx), x)
    right = (dp, lax.rem(ctx + 1, n_ctx), x)
    long_to = (dp, lax.rem(ctx + n_ctx - 4 * sign, n_ctx), x)
    short_to = (dp, lax.rem(ctx + n_ctx + 4 * sign, n_ctx), x)
    pair = (dp, ctx + 2 - 4 * yl, x)
    across = (lax.rem(dp + 2 * yl - 1 + n_dp, n_dp), ctx + 2 - 4 * yl, x)
    sib = (dp, ctx + 1 - 2 * core, x)
    xp = (dp, ctx, lax.rem(x + 1, n_x))
    xm = (dp, ctx, lax.rem(x + n_x - 1, n_x))

    def remote(src, dst, send, recv, device):
        return pltpu.make_async_remote_copy(
            src_ref=src, dst_ref=dst, send_sem=send, recv_sem=recv,
            device_id=device, device_id_type=MESH,
        )

    barrier = pltpu.get_barrier_semaphore()
    partners = (left, right, long_to, short_to, pair, across, sib, xp, xm)
    for device in partners:
        pl.semaphore_signal(barrier, inc=1, device_id=device, device_id_type=MESH)

    def shard(e, yy):
        zz = lax.rem(z + sign * e + n_z, n_z)
        return pl.ds(pl.multiple_of((zz * 4 + yy * 2 + core) * wrows, wrows), wrows)

    own_w = []
    for n in range(crosses):
        cols = pl.ds(n * HEAD_DIM, HEAD_DIM)
        for kv, src in enumerate((wk_hbm, wv_hbm)):
            own_w.append(pltpu.make_async_copy(
                src.at[:, cols], w.at[n, shard(0, yl), pl.ds(kv * HEAD_DIM, HEAD_DIM)], own_w_sem.at[n, kv]))
    copies = [
        pltpu.make_async_copy(docs_hbm, docs.at[1], local_sem.at[0]),
        pltpu.make_async_copy(q_hbm, qv, local_sem.at[1]),
        pltpu.make_async_copy(tq_hbm, tq.at[2], local_sem.at[2]),
    ]
    for h in range(heads):
        cols = pl.ds(h * HEAD_DIM, HEAD_DIM)
        copies.append(pltpu.make_async_copy(k_hbm.at[:, cols], kb.at[1, h], local_sem.at[3 + 2 * h]))
        copies.append(pltpu.make_async_copy(v_hbm.at[:, cols], vb.at[1, h], local_sem.at[4 + 2 * h]))
    for copy in own_w + copies:
        copy.start()
    for copy in own_w:
        copy.wait()

    pl.semaphore_wait(barrier, len(partners))

    sends = []

    def go(copy):
        copy.start()
        sends.append(copy)
        return copy

    sides = ((left, 2), (right, 0))
    halo, small = {}, {}
    for side, (device, slot) in enumerate(sides):
        small[side, 0] = go(remote(docs_hbm, docs.at[slot], small_s.at[side, 0], small_r.at[side, 0], device))

    def start_halo(h):
        cols = pl.ds(h * HEAD_DIM, HEAD_DIM)
        for side, (device, slot) in enumerate(sides):
            halo[side, 0, h] = go(remote(
                k_hbm.at[:, cols], kb.at[slot, h], halo_s.at[side, 0, h], halo_r.at[side, 0, h], device))
            halo[side, 1, h] = go(remote(
                v_hbm.at[:, cols], vb.at[slot, h], halo_s.at[side, 1, h], halo_r.at[side, 1, h], device))

    far_y = ((3, 1), (4, 1), (5, 1), (6, 1))
    zmove, ymove, smove = {}, {}, {}

    def send_z(ring, step, n):
        e = step - 1 if ring == 0 else 1 - step
        at = w.at[n, shard(e, yl)]
        zmove[ring, step, n] = go(remote(
            at, at, zs.at[ring, step - 1, n], zr.at[ring, step - 1, n], long_to if ring == 0 else short_to))

    def send_y(e, n):
        at = w.at[n, shard(e, yl)]
        there = (n_z - e) % n_z
        ymove[there, n] = go(remote(
            at, at, ys.at[there, n], yr.at[there, n], pair if (e, n) in far_y else across))

    def send_sib(parity, e, n):
        at = w.at[n, shard(e, yl if parity == 0 else 1 - yl)]
        smove[parity, e, n] = go(remote(at, at, ss.at[parity, e, n], sr.at[parity, e, n], sib))

    def arrive(ring, step, n):
        zmove[ring, step, n].wait_recv()
        e = step if ring == 0 else n_z - step
        if ring == 0 and (step < 4 or (step == 4 and n == 0)):
            send_z(0, step + 1, n)
        if ring == 1 and (step < 2 or (step == 2 and n == 1)):
            send_z(1, step + 1, n)
        send_y(e, n)
        send_sib(0, e, n)

    def come_y(e, n):
        ymove[e, n].wait_recv()
        send_sib(1, e, n)

    for n in range(crosses):
        send_z(0, 1, n)
        send_z(1, 1, n)
        send_y(0, n)
    for h in range(heads):
        start_halo(h)
    for n in range(crosses):
        send_sib(0, 0, n)
    for side, (device, slot) in enumerate(sides):
        small[side, 1] = go(remote(tq_hbm, tq.at[1 - side], small_s.at[side, 1], small_r.at[side, 1], device))

    for copy in copies:
        copy.wait()
    for side in range(2):
        small[side, 0].wait_recv()

    marks = [docs[slot].astype(F32) for slot in range(3)]
    own_col = column_of(marks[1], rows, 1)
    tgt_col = [column_of(marks[slot], tgts, rows // tgts) for slot in range(3)]
    side_col = jnp.concatenate([tgt_col[0], tgt_col[2]], axis=0)

    xmove, xfwd = {}, {}

    def attend(h):
        for side in range(2):
            for kv in range(2):
                halo[side, kv, h].wait_recv()
        query = qv[:, h * HEAD_DIM:(h + 1) * HEAD_DIM]
        scores = []
        for slot in range(3):
            raw = nt(query, kb[slot, h]) * SCALE
            scores.append(jnp.where(own_col == marks[slot], raw, NEG_FILL))
        top = jnp.max(jnp.maximum(jnp.maximum(scores[0], scores[1]), scores[2]), axis=1, keepdims=True)
        weights = [jnp.exp(s - top) for s in scores]
        total = jnp.sum(weights[0] + weights[1] + weights[2], axis=1, keepdims=True)
        summed = sum(nn(weights[slot].astype(BF16), vb[slot, h]) for slot in range(3))
        at = pl.ds(pl.multiple_of((x * heads + h) * HEAD_DIM, HEAD_DIM), HEAD_DIM)
        enc[:, at] = (summed / total).astype(BF16)
        for side, device in enumerate((xp, xm)):
            xmove[side, h] = go(remote(enc.at[:, at], enc.at[:, at], xs.at[side, h], xr.at[side, h], device))

    def hand_on(h):
        for side in range(2):
            xmove[side, h].wait_recv()
        side = h % 2
        source = lax.rem(x + n_x - 1, n_x) if side == 0 else lax.rem(x + 1, n_x)
        at = pl.ds(pl.multiple_of((source * heads + h) * HEAD_DIM, HEAD_DIM), HEAD_DIM)
        xfwd[h] = go(remote(enc.at[:, at], enc.at[:, at], xfs.at[h], xfr.at[h], (xp, xm)[side]))

    arrive(0, 1, 0)
    arrive(0, 1, 1)
    come_y(0, 0)
    attend(0)
    arrive(1, 1, 0)
    arrive(0, 2, 0)
    come_y(0, 1)
    arrive(0, 2, 1)
    arrive(1, 1, 1)
    hand_on(0)
    attend(1)
    come_y(7, 0)
    come_y(7, 1)
    come_y(1, 0)
    arrive(0, 3, 0)
    arrive(0, 3, 1)
    arrive(1, 2, 0)
    hand_on(1)
    attend(2)
    come_y(6, 0)
    arrive(0, 4, 0)
    arrive(1, 2, 1)
    arrive(0, 4, 1)
    hand_on(2)
    attend(3)
    come_y(6, 1)
    come_y(1, 1)
    arrive(0, 5, 0)
    come_y(5, 0)
    arrive(1, 3, 1)
    come_y(2, 0)
    hand_on(3)
    come_y(4, 0)
    come_y(3, 0)

    for h in range(heads):
        xfwd[h].wait_recv()

    def maps(n):
        for parity in range(2):
            for e in range(n_z):
                smove[parity, e, n].wait_recv()
        both = nn(enc[...], w[n]).astype(BF16)
        return both[:, :HEAD_DIM], both[:, HEAD_DIM:]

    def partial_sums(query, col, memory):
        raw = nt(query, memory[0]) * SCALE
        scores = jnp.where(col == marks[1], raw, NEG_FILL)
        top = jnp.max(scores, axis=1, keepdims=True)
        weights = jnp.exp(scores - top)
        total = jnp.sum(weights, axis=1, keepdims=True)
        return top, total, nn(weights.astype(BF16), memory[1])

    lane = lax.broadcasted_iota(jnp.int32, (tgts, 128), 1)
    cmove = {}

    def give(n, memory):
        query = tq[0:2, :, n * HEAD_DIM:(n + 1) * HEAD_DIM].reshape(2 * tgts, HEAD_DIM)
        top, total, summed = partial_sums(query, side_col, memory)
        for side in range(2):
            at = slice(side * tgts, (side + 1) * tgts)
            part_out[side, n, :, 0:HEAD_DIM] = summed[at]
            part_out[side, n, :, HEAD_DIM:] = jnp.where(lane == 0, top[at], total[at])
            cmove[side, n] = go(remote(
                part_out.at[side, n], part_in.at[1 - side, n], cs.at[side, n], cr.at[side, n], sides[side][0]))

    def merge(n, own):
        tops, totals, sums = [own[0]], [own[1]], [own[2]]
        for side in range(2):
            cmove[side, n].wait_recv()
            tops.append(part_in[1 - side, n, :, HEAD_DIM:HEAD_DIM + 1])
            totals.append(part_in[1 - side, n, :, HEAD_DIM + 1:HEAD_DIM + 2])
            sums.append(part_in[1 - side, n, :, 0:HEAD_DIM])
        most = jnp.maximum(jnp.maximum(tops[0], tops[1]), tops[2])
        factor = [jnp.exp(t - most) for t in tops]
        total = sum(f * t for f, t in zip(factor, totals))
        summed = sum(f * s for f, s in zip(factor, sums))
        out_ref[:, n * HEAD_DIM:(n + 1) * HEAD_DIM] = summed / total

    for side in range(2):
        small[side, 1].wait_recv()
    own = {}
    for n in range(crosses):
        if n == 1:
            for e in (7, 6, 5, 2, 4, 3):
                if (e, 1) not in [key[1:] for key in smove if key[0] == 1]:
                    come_y(e, 1)
        memory = maps(n)
        give(n, memory)
        own[n] = partial_sums(tq[2, :, n * HEAD_DIM:(n + 1) * HEAD_DIM], tgt_col[1], memory)
    for n in range(crosses):
        merge(n, own[n])

    for copy in sends:
        copy.wait_send()


def on_device(sizes, enc_query, enc_key, enc_value, doc_ids, key_map, value_map, tgt_query):
    rows, width = enc_key.shape
    heads = width // HEAD_DIM
    wrows, wcols = key_map.shape
    crosses = wcols // HEAD_DIM
    tgts = tgt_query.shape[0]
    n_z = sizes[1] // 4
    docs = doc_ids.reshape(1, rows)
    dma = pltpu.SemaphoreType.DMA
    any_spec = pl.BlockSpec(memory_space=pl.ANY)
    out = pl.pallas_call(
        functools.partial(kernel, sizes),
        out_shape=jax.ShapeDtypeStruct((tgts, wcols), F32),
        in_specs=[any_spec] * 7,
        out_specs=pl.BlockSpec(memory_space=pltpu.VMEM),
        scratch_shapes=[
            pltpu.VMEM((rows, width), BF16),
            pltpu.VMEM((3, heads, rows, HEAD_DIM), BF16),
            pltpu.VMEM((3, heads, rows, HEAD_DIM), BF16),
            pltpu.VMEM((3, 1, rows), jnp.int32),
            pltpu.VMEM((3, tgts, wcols), BF16),
            pltpu.VMEM((crosses, wrows * sizes[1], 2 * HEAD_DIM), BF16),
            pltpu.VMEM((rows, width * sizes[2]), BF16),
            pltpu.VMEM((2, crosses, tgts, HEAD_DIM + 128), F32),
            pltpu.VMEM((2, crosses, tgts, HEAD_DIM + 128), F32),
            dma((3 + 2 * heads,)),
            dma((crosses, 2)),
            dma((2, 2, heads)),
            dma((2, 2, heads)),
            dma((2, 2)),
            dma((2, 2)),
            dma((2, 5, crosses)),
            dma((2, 5, crosses)),
            dma((n_z, crosses)),
            dma((n_z, crosses)),
            dma((2, n_z, crosses)),
            dma((2, n_z, crosses)),
            dma((2, heads)),
            dma((2, heads)),
            dma((heads,)),
            dma((heads,)),
            dma((2, crosses)),
            dma((2, crosses)),
        ],
        compiler_params=pltpu.CompilerParams(
            collective_id=0, has_side_effects=True, vmem_limit_bytes=60 * 1024 * 1024
        ),
    )(enc_query, enc_key, enc_value, docs, key_map, value_map, tgt_query)
    return out.astype(BF16)


def solution(mesh):
    sizes = (mesh.shape["dp"], mesh.shape["ctx"], mesh.shape["head"])
    in_specs = (
        P(("dp", "ctx"), "head"),
        P(("dp", "ctx"), "head"),
        P(("dp", "ctx"), "head"),
        P(("dp", "ctx")),
        P("ctx", "head"),
        P("ctx", "head"),
        P(("dp", "ctx"), "head"),
    )
    return jax.shard_map(
        functools.partial(on_device, sizes),
        mesh=mesh,
        in_specs=in_specs,
        out_specs=P(("dp", "ctx"), "head"),
        check_vma=False,
    )
```

```python
import functools

import jax
import jax.numpy as jnp
from jax import lax
from jax.experimental import pallas as pl
from jax.experimental.pallas import tpu as pltpu
from jax.sharding import PartitionSpec as P

MESH = pl.DeviceIdType.MESH
HEAD_DIM = 256
NEG_FILL = -1e30
SCALE = HEAD_DIM ** (-0.5)
F32 = jnp.float32
BF16 = jnp.bfloat16


def nt(a, b):
    return lax.dot_general(a, b, (((1,), (1,)), ((), ())), preferred_element_type=F32)


def nn(a, b):
    return lax.dot_general(a, b, (((1,), (0,)), ((), ())), preferred_element_type=F32)


def column_of(row, count, step):
    n = row.shape[1]
    i = lax.broadcasted_iota(jnp.int32, (count, n), 0)
    j = lax.broadcasted_iota(jnp.int32, (count, n), 1)
    return jnp.sum(jnp.where(j == step * i, row, 0.0), axis=1, keepdims=True)


def kernel(
    sizes,
    q_hbm,
    k_hbm,
    v_hbm,
    docs_hbm,
    wk_hbm,
    wv_hbm,
    tq_hbm,
    out_ref,
    qv,
    kb,
    vb,
    docs,
    tq,
    w,
    enc,
    part_out,
    part_in,
    local_sem,
    own_w_sem,
    halo_s,
    halo_r,
    small_s,
    small_r,
    zs,
    zr,
    ys,
    yr,
    ss,
    sr,
    xs,
    xr,
    xfs,
    xfr,
    cs,
    cr,
    os_,
    or_,
):
    n_dp, n_ctx, n_x = sizes
    n_z = n_ctx // 4
    dp = lax.axis_index("dp")
    ctx = lax.axis_index("ctx")
    x = lax.axis_index("head")
    core = lax.rem(ctx, 2)
    yl = lax.rem(ctx // 2, 2)
    z = ctx // 4
    sign = 1 - 2 * yl

    heads = k_hbm.shape[1] // HEAD_DIM
    rows = k_hbm.shape[0]
    tgts = tq_hbm.shape[0]
    crosses = wk_hbm.shape[1] // HEAD_DIM
    wrows = wk_hbm.shape[0]

    left = (dp, lax.rem(ctx + n_ctx - 1, n_ctx), x)
    right = (dp, lax.rem(ctx + 1, n_ctx), x)
    long_to = (dp, lax.rem(ctx + n_ctx - 4 * sign, n_ctx), x)
    short_to = (dp, lax.rem(ctx + n_ctx + 4 * sign, n_ctx), x)
    pair = (dp, ctx + 2 - 4 * yl, x)
    across = (lax.rem(dp + 2 * yl - 1 + n_dp, n_dp), ctx + 2 - 4 * yl, x)
    sib = (dp, ctx + 1 - 2 * core, x)
    xp = (dp, ctx, lax.rem(x + 1, n_x))
    xm = (dp, ctx, lax.rem(x + n_x - 1, n_x))

    def remote(src, dst, send, recv, device):
        return pltpu.make_async_remote_copy(
            src_ref=src, dst_ref=dst, send_sem=send, recv_sem=recv,
            device_id=device, device_id_type=MESH,
        )

    barrier = pltpu.get_barrier_semaphore()
    partners = (left, right, long_to, short_to, pair, across, sib, xp, xm)
    for device in partners:
        pl.semaphore_signal(barrier, inc=1, device_id=device, device_id_type=MESH)

    def shard(e, yy):
        zz = lax.rem(z + sign * e + n_z, n_z)
        return pl.ds(pl.multiple_of((zz * 4 + yy * 2 + core) * wrows, wrows), wrows)

    own_w = []
    for n in range(crosses):
        cols = pl.ds(n * HEAD_DIM, HEAD_DIM)
        for kv, src in enumerate((wk_hbm, wv_hbm)):
            own_w.append(pltpu.make_async_copy(
                src.at[:, cols], w.at[n, shard(0, yl), pl.ds(kv * HEAD_DIM, HEAD_DIM)], own_w_sem.at[n, kv]))
    copies = [
        pltpu.make_async_copy(docs_hbm, docs.at[1], local_sem.at[0]),
        pltpu.make_async_copy(q_hbm, qv, local_sem.at[1]),
        pltpu.make_async_copy(tq_hbm, tq.at[2], local_sem.at[2]),
    ]
    for h in range(heads):
        cols = pl.ds(h * HEAD_DIM, HEAD_DIM)
        copies.append(pltpu.make_async_copy(k_hbm.at[:, cols], kb.at[1, h], local_sem.at[3 + 2 * h]))
        copies.append(pltpu.make_async_copy(v_hbm.at[:, cols], vb.at[1, h], local_sem.at[4 + 2 * h]))
    for copy in own_w + copies:
        copy.start()
    pl.semaphore_wait(barrier, len(partners))

    sends = []

    def go(copy):
        copy.start()
        sends.append(copy)
        return copy

    sides = ((left, 2), (right, 0))
    halo, small = {}, {}
    for side, (device, slot) in enumerate(sides):
        small[side, 0] = go(remote(docs_hbm, docs.at[slot], small_s.at[side, 0], small_r.at[side, 0], device))

    def start_halo(h):
        cols = pl.ds(h * HEAD_DIM, HEAD_DIM)
        for side, (device, slot) in enumerate(sides):
            halo[side, 0, h] = go(remote(
                k_hbm.at[:, cols], kb.at[slot, h], halo_s.at[side, 0, h], halo_r.at[side, 0, h], device))
            halo[side, 1, h] = go(remote(
                v_hbm.at[:, cols], vb.at[slot, h], halo_s.at[side, 1, h], halo_r.at[side, 1, h], device))

    far_y = ((4, 0), (5, 0), (5, 1))
    by_ring = ((6, 0), (6, 1), (4, 1))
    zmove, ymove, smove, omove = {}, {}, {}, {}

    def send_z(ring, step, n):
        e = step - 1 if ring == 0 else 1 - step
        at = w.at[n, shard(e, yl)]
        zmove[ring, step, n] = go(remote(
            at, at, zs.at[ring, step - 1, n], zr.at[ring, step - 1, n], long_to if ring == 0 else short_to))

    def send_y(e, n):
        if (e, n) in by_ring:
            return
        at = w.at[n, shard(e, yl)]
        there = (n_z - e) % n_z
        ymove[there, n] = go(remote(
            at, at, ys.at[there, n], yr.at[there, n], pair if (e, n) in far_y else across))

    def send_sib(parity, e, n):
        at = w.at[n, shard(e, yl if parity == 0 else 1 - yl)]
        smove[parity, e, n] = go(remote(at, at, ss.at[parity, e, n], sr.at[parity, e, n], sib))

    def arrive(ring, step, n):
        zmove[ring, step, n].wait_recv()
        e = step if ring == 0 else n_z - step
        if ring == 0 and (step < 4 or (step == 4 and n == 0)):
            send_z(0, step + 1, n)
        if ring == 1 and (step < 2 or (step == 2 and n == 1)):
            send_z(1, step + 1, n)
        send_y(e, n)
        send_sib(0, e, n)

    def send_o(ring, n):
        at = w.at[n, shard(1 if ring == 0 else 5, 1 - yl)]
        omove[ring, n] = go(remote(
            at, at, os_.at[ring, n], or_.at[ring, n], long_to if ring == 0 else short_to))

    def come_o(ring, n):
        omove[ring, n].wait_recv()
        send_sib(1, 2 if ring == 0 else 4, n)

    def come_y(e, n):
        ymove[e, n].wait_recv()
        send_sib(1, e, n)

    start_halo(0)
    for copy in own_w:
        copy.wait()
    for n in range(crosses):
        send_z(0, 1, n)
        send_z(1, 1, n)
        send_y(0, n)
    for h in range(1, heads):
        start_halo(h)
    for n in range(crosses):
        send_sib(0, 0, n)
    for side, (device, slot) in enumerate(sides):
        small[side, 1] = go(remote(tq_hbm, tq.at[1 - side], small_s.at[side, 1], small_r.at[side, 1], device))

    for copy in copies:
        copy.wait()
    for side in range(2):
        small[side, 0].wait_recv()

    marks = [docs[slot].astype(F32) for slot in range(3)]
    own_col = column_of(marks[1], rows, 1)
    tgt_col = [column_of(marks[slot], tgts, rows // tgts) for slot in range(3)]
    side_col = jnp.concatenate([tgt_col[0], tgt_col[2]], axis=0)

    xmove, xfwd = {}, {}

    def half_rows(half):
        return pl.ds(half * (rows // 2), rows // 2)

    def attend(h):
        for side in range(2):
            for kv in range(2):
                halo[side, kv, h].wait_recv()
        query = qv[:, h * HEAD_DIM:(h + 1) * HEAD_DIM]
        scores = []
        for slot in range(3):
            raw = nt(query, kb[slot, h]) * SCALE
            scores.append(jnp.where(own_col == marks[slot], raw, NEG_FILL))
        top = jnp.max(jnp.maximum(jnp.maximum(scores[0], scores[1]), scores[2]), axis=1, keepdims=True)
        weights = [jnp.exp(s - top) for s in scores]
        total = jnp.sum(weights[0] + weights[1] + weights[2], axis=1, keepdims=True)
        summed = sum(nn(weights[slot].astype(BF16), vb[slot, h]) for slot in range(3))
        at = pl.ds(pl.multiple_of((x * heads + h) * HEAD_DIM, HEAD_DIM), HEAD_DIM)
        enc[:, at] = (summed / total).astype(BF16)
        for part in range(2):
            for side, device in enumerate((xp, xm)):
                piece = enc.at[half_rows(part if side == 0 else 1 - part), at]
                xmove[side, h, part] = go(remote(piece, piece, xs.at[side, h, part], xr.at[side, h, part], device))

    def hand_on(h):
        for side, device in enumerate((xp, xm)):
            xmove[side, h, 0].wait_recv()
            source = lax.rem(x + n_x - 1, n_x) if side == 0 else lax.rem(x + 1, n_x)
            at = pl.ds(pl.multiple_of((source * heads + h) * HEAD_DIM, HEAD_DIM), HEAD_DIM)
            piece = enc.at[half_rows(side), at]
            xfwd[side, h] = go(remote(piece, piece, xfs.at[side, h], xfr.at[side, h], device))

    arrive(0, 1, 0)
    come_y(0, 0)
    arrive(0, 1, 1)
    attend(0)
    come_y(0, 1)
    arrive(1, 1, 0)
    arrive(0, 2, 0)
    come_y(7, 0)
    arrive(0, 2, 1)
    arrive(1, 1, 1)
    attend(1)
    hand_on(0)
    come_y(7, 1)
    arrive(0, 3, 0)
    arrive(0, 3, 1)
    arrive(1, 2, 0)
    attend(2)
    hand_on(1)
    come_y(1, 0)
    come_y(6, 0)
    arrive(0, 4, 0)
    send_o(0, 0)
    arrive(0, 4, 1)
    arrive(1, 2, 1)
    attend(3)
    hand_on(2)
    come_y(6, 1)
    come_y(1, 1)
    send_o(0, 1)
    arrive(0, 5, 0)
    come_y(4, 0)
    come_y(5, 0)
    come_y(5, 1)
    send_o(1, 1)
    arrive(1, 3, 1)
    hand_on(3)
    come_o(0, 0)
    come_y(3, 0)
    come_o(0, 1)
    come_o(1, 1)

    for h in range(heads):
        for side in range(2):
            xmove[side, h, 1].wait_recv()
            xfwd[side, h].wait_recv()

    def maps(n):
        for parity in range(2):
            for e in range(n_z):
                smove[parity, e, n].wait_recv()
        both = nn(enc[...], w[n]).astype(BF16)
        return both[:, :HEAD_DIM], both[:, HEAD_DIM:]

    def partial_sums(query, col, memory):
        raw = nt(query, memory[0]) * SCALE
        scores = jnp.where(col == marks[1], raw, NEG_FILL)
        top = jnp.max(scores, axis=1, keepdims=True)
        weights = jnp.exp(scores - top)
        total = jnp.sum(weights, axis=1, keepdims=True)
        return top, total, nn(weights.astype(BF16), memory[1])

    diagonal = lax.broadcasted_iota(jnp.int32, (tgts, HEAD_DIM), 0) == lax.broadcasted_iota(
        jnp.int32, (tgts, HEAD_DIM), 1)
    first_row = lax.broadcasted_iota(jnp.int32, (8, HEAD_DIM), 0) == 0
    cmove = {}

    def row_of(column):
        return jnp.sum(jnp.where(diagonal, column, 0.0), axis=0, keepdims=True)

    def give(n, memory):
        query = tq[0:2, :, n * HEAD_DIM:(n + 1) * HEAD_DIM].reshape(2 * tgts, HEAD_DIM)
        top, total, summed = partial_sums(query, side_col, memory)
        for side in range(2):
            at = slice(side * tgts, (side + 1) * tgts)
            part_out[side, n, 0:tgts] = summed[at]
            part_out[side, n, tgts:] = jnp.where(first_row, row_of(top[at]), row_of(total[at]))
            cmove[side, n] = go(remote(
                part_out.at[side, n], part_in.at[1 - side, n], cs.at[side, n], cr.at[side, n], sides[side][0]))

    def merge(n, own):
        tops, totals, sums = [own[0]], [own[1]], [own[2]]
        for side in range(2):
            cmove[side, n].wait_recv()
            tops.append(column_of(part_in[1 - side, n, tgts:tgts + 1], tgts, 1))
            totals.append(column_of(part_in[1 - side, n, tgts + 1:tgts + 2], tgts, 1))
            sums.append(part_in[1 - side, n, 0:tgts])
        most = jnp.maximum(jnp.maximum(tops[0], tops[1]), tops[2])
        factor = [jnp.exp(t - most) for t in tops]
        total = sum(f * t for f, t in zip(factor, totals))
        summed = sum(f * s for f, s in zip(factor, sums))
        out_ref[:, n * HEAD_DIM:(n + 1) * HEAD_DIM] = summed / total

    for side in range(2):
        small[side, 1].wait_recv()
    memory = {}
    for n in range(crosses):
        if n == 1:
            come_y(3, 1)
        memory[n] = maps(n)
        give(n, memory[n])
    own = [
        partial_sums(tq[2, :, n * HEAD_DIM:(n + 1) * HEAD_DIM], tgt_col[1], memory[n]) for n in range(crosses)
    ]
    for n in range(crosses):
        merge(n, own[n])

    for copy in sends:
        copy.wait_send()


def on_device(sizes, enc_query, enc_key, enc_value, doc_ids, key_map, value_map, tgt_query):
    rows, width = enc_key.shape
    heads = width // HEAD_DIM
    wrows, wcols = key_map.shape
    crosses = wcols // HEAD_DIM
    tgts = tgt_query.shape[0]
    n_z = sizes[1] // 4
    docs = doc_ids.reshape(1, rows)
    dma = pltpu.SemaphoreType.DMA
    any_spec = pl.BlockSpec(memory_space=pl.ANY)
    out = pl.pallas_call(
        functools.partial(kernel, sizes),
        out_shape=jax.ShapeDtypeStruct((tgts, wcols), F32),
        in_specs=[any_spec] * 7,
        out_specs=pl.BlockSpec(memory_space=pltpu.VMEM),
        scratch_shapes=[
            pltpu.VMEM((rows, width), BF16),
            pltpu.VMEM((3, heads, rows, HEAD_DIM), BF16),
            pltpu.VMEM((3, heads, rows, HEAD_DIM), BF16),
            pltpu.VMEM((3, 1, rows), jnp.int32),
            pltpu.VMEM((3, tgts, wcols), BF16),
            pltpu.VMEM((crosses, wrows * sizes[1], 2 * HEAD_DIM), BF16),
            pltpu.VMEM((rows, width * sizes[2]), BF16),
            pltpu.VMEM((2, crosses, tgts + 8, HEAD_DIM), F32),
            pltpu.VMEM((2, crosses, tgts + 8, HEAD_DIM), F32),
            dma((3 + 2 * heads,)),
            dma((crosses, 2)),
            dma((2, 2, heads)),
            dma((2, 2, heads)),
            dma((2, 2)),
            dma((2, 2)),
            dma((2, 5, crosses)),
            dma((2, 5, crosses)),
            dma((n_z, crosses)),
            dma((n_z, crosses)),
            dma((2, n_z, crosses)),
            dma((2, n_z, crosses)),
            dma((2, heads, 2)),
            dma((2, heads, 2)),
            dma((2, heads)),
            dma((2, heads)),
            dma((2, crosses)),
            dma((2, crosses)),
            dma((2, crosses)),
            dma((2, crosses)),
        ],
        compiler_params=pltpu.CompilerParams(
            collective_id=0, has_side_effects=True, vmem_limit_bytes=60 * 1024 * 1024
        ),
    )(enc_query, enc_key, enc_value, docs, key_map, value_map, tgt_query)
    return out.astype(BF16)


def solution(mesh):
    sizes = (mesh.shape["dp"], mesh.shape["ctx"], mesh.shape["head"])
    in_specs = (
        P(("dp", "ctx"), "head"),
        P(("dp", "ctx"), "head"),
        P(("dp", "ctx"), "head"),
        P(("dp", "ctx")),
        P("ctx", "head"),
        P("ctx", "head"),
        P(("dp", "ctx"), "head"),
    )
    return jax.shard_map(
        functools.partial(on_device, sizes),
        mesh=mesh,
        in_specs=in_specs,
        out_specs=P(("dp", "ctx"), "head"),
        check_vma=False,
    )
```

```python
import functools

import jax
import jax.numpy as jnp
from jax import lax
from jax.experimental import pallas as pl
from jax.experimental.pallas import tpu as pltpu
from jax.sharding import PartitionSpec as P

MESH = pl.DeviceIdType.MESH
HEAD_DIM = 256
NEG_FILL = -1e30
SCALE = HEAD_DIM ** (-0.5)
F32 = jnp.float32
BF16 = jnp.bfloat16


def nt(a, b):
    return lax.dot_general(a, b, (((1,), (1,)), ((), ())), preferred_element_type=F32)


def nn(a, b):
    return lax.dot_general(a, b, (((1,), (0,)), ((), ())), preferred_element_type=F32)


def column_of(row, count, step):
    n = row.shape[1]
    i = lax.broadcasted_iota(jnp.int32, (count, n), 0)
    j = lax.broadcasted_iota(jnp.int32, (count, n), 1)
    return jnp.sum(jnp.where(j == step * i, row, 0.0), axis=1, keepdims=True)


def kernel(
    sizes,
    q_hbm,
    k_hbm,
    v_hbm,
    docs_hbm,
    wk_hbm,
    wv_hbm,
    tq_hbm,
    out_ref,
    qv,
    kb,
    vb,
    docs,
    tq,
    w,
    enc,
    acc,
    part_out,
    part_in,
    local_sem,
    halo_s,
    halo_r,
    small_s,
    small_r,
    map_s,
    z_r,
    y_r,
    o_r,
    sib_r,
    x_s,
    x_r,
    part_s,
    part_r,
):
    n_dp, n_ctx, n_x = sizes
    n_z = n_ctx // 4
    dp = lax.axis_index("dp")
    ctx = lax.axis_index("ctx")
    x = lax.axis_index("head")
    core = lax.rem(ctx, 2)
    yl = lax.rem(ctx // 2, 2)
    z = ctx // 4
    sign = 1 - 2 * yl

    heads = k_hbm.shape[1] // HEAD_DIM
    rows = k_hbm.shape[0]
    tgts = tq_hbm.shape[0]
    crosses = wk_hbm.shape[1] // HEAD_DIM
    wrows = wk_hbm.shape[0]

    left = (dp, lax.rem(ctx + n_ctx - 1, n_ctx), x)
    right = (dp, lax.rem(ctx + 1, n_ctx), x)
    long_to = (dp, lax.rem(ctx + n_ctx - 4 * sign, n_ctx), x)
    short_to = (dp, lax.rem(ctx + n_ctx + 4 * sign, n_ctx), x)
    pair = (dp, ctx + 2 - 4 * yl, x)
    across = (lax.rem(dp + 2 * yl - 1 + n_dp, n_dp), ctx + 2 - 4 * yl, x)
    sib = (dp, ctx + 1 - 2 * core, x)
    xp = (dp, ctx, lax.rem(x + 1, n_x))
    xm = (dp, ctx, lax.rem(x + n_x - 1, n_x))

    def remote(src, dst, send, recv, device):
        return pltpu.make_async_remote_copy(
            src_ref=src, dst_ref=dst, send_sem=send, recv_sem=recv,
            device_id=device, device_id_type=MESH,
        )

    def settle(ref, sem):
        pltpu.make_async_copy(ref, ref, sem).wait()

    def settle_rows(count, sem):
        settle(w.at[0, pl.ds(0, count)], sem)

    barrier = pltpu.get_barrier_semaphore()
    partners = (left, right, long_to, short_to, pair, across, sib, xp, xm)
    for device in partners:
        pl.semaphore_signal(barrier, inc=1, device_id=device, device_id_type=MESH)

    def place(parity, e):
        return parity * n_z + (e + 3) % n_z

    def shard(parity, e):
        return pl.ds(pl.multiple_of(place(parity, e) * HEAD_DIM + core * wrows, wrows), wrows)

    own_w = []
    for n in range(crosses):
        cols = pl.ds(n * HEAD_DIM, HEAD_DIM)
        for kv, src in enumerate((wk_hbm, wv_hbm)):
            own_w.append(pltpu.make_async_copy(
                src.at[:, cols], w.at[n, shard(0, 0), pl.ds(kv * HEAD_DIM, HEAD_DIM)], local_sem.at[4]))
    copies = [
        pltpu.make_async_copy(docs_hbm, docs.at[1], local_sem.at[0]),
        pltpu.make_async_copy(q_hbm, qv, local_sem.at[1]),
        pltpu.make_async_copy(tq_hbm, tq.at[2], local_sem.at[2]),
    ]
    for h in range(heads):
        cols = pl.ds(h * HEAD_DIM, HEAD_DIM)
        copies.append(pltpu.make_async_copy(k_hbm.at[:, cols], kb.at[1, h], local_sem.at[3]))
        copies.append(pltpu.make_async_copy(v_hbm.at[:, cols], vb.at[1, h], local_sem.at[3]))
    for copy in own_w:
        copy.start()
    pl.semaphore_wait(barrier, len(partners))

    counts = {"map": 0, "sib": 0, "x": 0}

    def go(copy, kind=None):
        copy.start()
        if kind:
            counts[kind] += 1

    sides = ((left, 2), (right, 0))
    for side, (device, slot) in enumerate(sides):
        go(remote(docs_hbm, docs.at[slot], small_s.at[0], small_r.at[0], device))

    def start_halo(h):
        cols = pl.ds(h * HEAD_DIM, HEAD_DIM)
        for side, (device, slot) in enumerate(sides):
            go(remote(k_hbm.at[:, cols], kb.at[slot, h], halo_s.at[0], halo_r.at[h], device))
            go(remote(v_hbm.at[:, cols], vb.at[slot, h], halo_s.at[0], halo_r.at[h], device))

    far_y = ((2, 1), (4, 0), (5, 0))
    by_ring = ((6, 0), (6, 1), (4, 1))
    last = (2, 3, 4)
    z_pieces = [(ring, step, n) for ring, far in ((0, 5), (1, 3)) for step in range(1, far + 1)
                for n in range(crosses) if step < far or n == ring]
    y_pieces = [(e, n) for e in range(n_z) for n in range(crosses) if ((n_z - e) % n_z, n) not in by_ring]
    o_pieces = [(0, 0), (0, 1), (1, 1)]

    def send_z(ring, step, n):
        e = step - 1 if ring == 0 else 1 - step
        there = step if ring == 0 else n_z - step
        src, dst = w.at[n, shard(0, e)], w.at[n, shard(0, there)]
        go(remote(
            src, dst, map_s.at[0], z_r.at[z_pieces.index((ring, step, n))],
            long_to if ring == 0 else short_to), "map")

    def send_y(e, n):
        if (e, n) in by_ring:
            return
        there = (n_z - e) % n_z
        src, dst = w.at[n, shard(0, e)], w.at[n, shard(1, there)]
        go(remote(
            src, dst, map_s.at[0], y_r.at[y_pieces.index((there, n))],
            pair if (e, n) in far_y else across), "map")

    def send_sib(parity, e, n):
        at = w.at[n, shard(parity, e)]
        group = 1 if parity == 1 and e in last else 0
        go(remote(at, at, map_s.at[1], sib_r.at[n, group], sib), "sib")

    def arrive(ring, step, n):
        settle_rows(wrows, z_r.at[z_pieces.index((ring, step, n))])
        e = step if ring == 0 else n_z - step
        if ring == 0 and (step < 4 or (step == 4 and n == 0)):
            send_z(0, step + 1, n)
        if ring == 1 and (step < 2 or (step == 2 and n == 1)):
            send_z(1, step + 1, n)
        send_y(e, n)
        send_sib(0, e, n)

    def send_o(ring, n):
        src = w.at[n, shard(1, 1 if ring == 0 else 5)]
        dst = w.at[n, shard(1, 2 if ring == 0 else 4)]
        go(remote(
            src, dst, map_s.at[0], o_r.at[o_pieces.index((ring, n))],
            long_to if ring == 0 else short_to), "map")

    def come_o(ring, n):
        settle_rows(wrows, o_r.at[o_pieces.index((ring, n))])
        send_sib(1, 2 if ring == 0 else 4, n)

    def come_y(e, n):
        settle_rows(wrows, y_r.at[y_pieces.index((e, n))])
        send_sib(1, e, n)

    start_halo(0)
    for copy in copies:
        copy.start()
    settle_rows(crosses * wrows, local_sem.at[4])
    for n in range(crosses):
        send_z(0, 1, n)
        send_z(1, 1, n)
        send_y(0, n)
    for h in range(1, heads):
        start_halo(h)
    for n in range(crosses):
        send_sib(0, 0, n)
    for side, (device, slot) in enumerate(sides):
        go(remote(tq_hbm, tq.at[1 - side], small_s.at[1], small_r.at[1], device))

    for copy in copies[:3]:
        copy.wait()
    settle_rows(2 * heads * rows // 2, local_sem.at[3])
    settle(docs.at[0:2], small_r.at[0])

    marks = [docs[slot].astype(F32) for slot in range(3)]
    own_col = column_of(marks[1], rows, 1)
    tgt_col = [column_of(marks[slot], tgts, rows // tgts) for slot in range(3)]
    side_col = jnp.concatenate([tgt_col[0], tgt_col[2]], axis=0)

    def enc_cols(at_x, h):
        e = lax.rem(sign * (at_x * 2 + h // 2 - z) + 2 * n_z + 3, n_z)
        parity = yl if h % 2 == 0 else 1 - yl
        return pl.ds(pl.multiple_of((parity * n_z + e) * HEAD_DIM, HEAD_DIM), HEAD_DIM)

    def half_rows(half):
        return pl.ds(half * (rows // 2), rows // 2)

    def attend(h):
        settle_rows(2 * rows, halo_r.at[h])
        query = qv[:, h * HEAD_DIM:(h + 1) * HEAD_DIM]
        scores = []
        for slot in range(3):
            raw = nt(query, kb[slot, h]) * SCALE
            scores.append(jnp.where(own_col == marks[slot], raw, NEG_FILL))
        top = jnp.max(jnp.maximum(jnp.maximum(scores[0], scores[1]), scores[2]), axis=1, keepdims=True)
        weights = [jnp.exp(s - top) for s in scores]
        total = jnp.sum(weights[0] + weights[1] + weights[2], axis=1, keepdims=True)
        summed = sum(nn(weights[slot].astype(BF16), vb[slot, h]) for slot in range(3))
        at = enc_cols(x, h)
        enc[:, at] = (summed / total).astype(BF16)
        for part in range(2):
            for side, device in enumerate((xp, xm)):
                piece = enc.at[half_rows(part if side == 0 else 1 - part), at]
                go(remote(piece, piece, x_s.at[0], x_r.at[h if part == 0 else heads], device), "x")

    def hand_on(h):
        settle_rows(rows // 2, x_r.at[h])
        for side, device in enumerate((xp, xm)):
            source = lax.rem(x + n_x - 1, n_x) if side == 0 else lax.rem(x + 1, n_x)
            at = enc_cols(source, h)
            piece = enc.at[half_rows(side), at]
            go(remote(piece, piece, x_s.at[0], x_r.at[heads], device), "x")

    arrive(0, 1, 0)
    come_y(0, 0)
    arrive(0, 1, 1)
    attend(0)
    come_y(0, 1)
    arrive(1, 1, 0)
    arrive(0, 2, 0)
    come_y(7, 0)
    arrive(0, 2, 1)
    arrive(1, 1, 1)
    attend(1)
    hand_on(0)
    come_y(7, 1)
    arrive(0, 3, 0)
    arrive(0, 3, 1)
    arrive(1, 2, 0)
    attend(2)
    hand_on(1)
    come_y(1, 0)
    come_y(6, 0)
    arrive(0, 4, 0)
    send_o(0, 0)
    arrive(0, 4, 1)
    arrive(1, 2, 1)
    attend(3)
    hand_on(2)
    come_y(1, 1)
    send_o(0, 1)
    arrive(0, 5, 0)
    come_y(5, 0)
    come_y(5, 1)
    send_o(1, 1)
    hand_on(3)
    arrive(1, 3, 1)
    come_y(6, 1)
    come_o(0, 0)
    come_y(4, 0)

    settle_rows(heads * rows, x_r.at[heads])

    split = (2 * n_z - len(last)) * HEAD_DIM

    def maps_most(n):
        settle_rows((2 * n_z - len(last)) * wrows, sib_r.at[n, 0])
        acc[n] = nn(enc[:, :split], w[n, :split])

    def maps_rest(n):
        settle_rows(len(last) * wrows, sib_r.at[n, 1])
        both = (acc[n] + nn(enc[:, split:], w[n, split:])).astype(BF16)
        return both[:, :HEAD_DIM], both[:, HEAD_DIM:]

    def partial_sums(query, col, memory):
        raw = nt(query, memory[0]) * SCALE
        scores = jnp.where(col == marks[1], raw, NEG_FILL)
        top = jnp.max(scores, axis=1, keepdims=True)
        weights = jnp.exp(scores - top)
        total = jnp.sum(weights, axis=1, keepdims=True)
        return top, total, nn(weights.astype(BF16), memory[1])

    diagonal = lax.broadcasted_iota(jnp.int32, (tgts, HEAD_DIM), 0) == lax.broadcasted_iota(
        jnp.int32, (tgts, HEAD_DIM), 1)
    first_row = lax.broadcasted_iota(jnp.int32, (8, HEAD_DIM), 0) == 0

    def row_of(column):
        return jnp.sum(jnp.where(diagonal, column, 0.0), axis=0, keepdims=True)

    def give(n, memory):
        query = tq[0:2, :, n * HEAD_DIM:(n + 1) * HEAD_DIM].reshape(2 * tgts, HEAD_DIM)
        top, total, summed = partial_sums(query, side_col, memory)
        for side in range(2):
            at = slice(side * tgts, (side + 1) * tgts)
            part_out[side, n, 0:tgts] = summed[at]
            part_out[side, n, tgts:] = jnp.where(first_row, row_of(top[at]), row_of(total[at]))
            go(remote(part_out.at[side, n], part_in.at[1 - side, n], part_s.at[0], part_r.at[n], sides[side][0]))

    def merge(n, own):
        settle(part_in.at[:, n], part_r.at[n])
        tops, totals, sums = [own[0]], [own[1]], [own[2]]
        for side in range(2):
            tops.append(column_of(part_in[1 - side, n, tgts:tgts + 1], tgts, 1))
            totals.append(column_of(part_in[1 - side, n, tgts + 1:tgts + 2], tgts, 1))
            sums.append(part_in[1 - side, n, 0:tgts])
        most = jnp.maximum(jnp.maximum(tops[0], tops[1]), tops[2])
        factor = [jnp.exp(t - most) for t in tops]
        total = sum(f * t for f, t in zip(factor, totals))
        summed = sum(f * s for f, s in zip(factor, sums))
        out_ref[:, n * HEAD_DIM:(n + 1) * HEAD_DIM] = summed / total

    settle(tq.at[0:2], small_r.at[1])
    maps_most(0)
    come_y(3, 0)
    come_o(0, 1)
    come_o(1, 1)
    come_y(3, 1)
    maps_most(1)
    memory = {}
    for n in range(crosses):
        memory[n] = maps_rest(n)
        give(n, memory[n])
    own = [
        partial_sums(tq[2, :, n * HEAD_DIM:(n + 1) * HEAD_DIM], tgt_col[1], memory[n]) for n in range(crosses)
    ]
    for n in range(crosses):
        merge(n, own[n])

    settle(docs.at[0:2], small_s.at[0])
    settle(tq.at[0:2], small_s.at[1])
    settle(part_out, part_s.at[0])
    settle_rows(2 * heads * rows, halo_s.at[0])
    settle_rows(counts["x"] * rows // 4, x_s.at[0])
    settle_rows(counts["map"] * wrows, map_s.at[0])
    settle_rows(counts["sib"] * wrows, map_s.at[1])


def on_device(sizes, enc_query, enc_key, enc_value, doc_ids, key_map, value_map, tgt_query):
    rows, width = enc_key.shape
    heads = width // HEAD_DIM
    wrows, wcols = key_map.shape
    crosses = wcols // HEAD_DIM
    tgts = tgt_query.shape[0]
    n_z = sizes[1] // 4
    docs = doc_ids.reshape(1, rows)
    dma = pltpu.SemaphoreType.DMA
    any_spec = pl.BlockSpec(memory_space=pl.ANY)
    out = pl.pallas_call(
        functools.partial(kernel, sizes),
        out_shape=pltpu.VMEM((tgts, wcols), F32),
        in_specs=[any_spec] * 7,
        out_specs=pl.BlockSpec(memory_space=pltpu.VMEM),
        scratch_shapes=[
            pltpu.VMEM((rows, width), BF16),
            pltpu.VMEM((3, heads, rows, HEAD_DIM), BF16),
            pltpu.VMEM((3, heads, rows, HEAD_DIM), BF16),
            pltpu.VMEM((3, 1, rows), jnp.int32),
            pltpu.VMEM((3, tgts, wcols), BF16),
            pltpu.VMEM((crosses, wrows * sizes[1], 2 * HEAD_DIM), BF16),
            pltpu.VMEM((rows, width * sizes[2]), BF16),
            pltpu.VMEM((crosses, rows, 2 * HEAD_DIM), F32),
            pltpu.VMEM((2, crosses, tgts + 8, HEAD_DIM), F32),
            pltpu.VMEM((2, crosses, tgts + 8, HEAD_DIM), F32),
            dma((5,)),
            dma((1,)),
            dma((heads,)),
            dma((2,)),
            dma((2,)),
            dma((2,)),
            dma((14,)),
            dma((13,)),
            dma((3,)),
            dma((crosses, 2)),
            dma((1,)),
            dma((heads + 1,)),
            dma((1,)),
            dma((crosses,)),
        ],
        compiler_params=pltpu.CompilerParams(
            collective_id=0, has_side_effects=True, vmem_limit_bytes=60 * 1024 * 1024
        ),
    )(enc_query, enc_key, enc_value, docs, key_map, value_map, tgt_query)
    return out.astype(BF16)


def solution(mesh):
    sizes = (mesh.shape["dp"], mesh.shape["ctx"], mesh.shape["head"])
    in_specs = (
        P(("dp", "ctx"), "head"),
        P(("dp", "ctx"), "head"),
        P(("dp", "ctx"), "head"),
        P(("dp", "ctx")),
        P("ctx", "head"),
        P("ctx", "head"),
        P(("dp", "ctx"), "head"),
    )
    return jax.shard_map(
        functools.partial(on_device, sizes),
        mesh=mesh,
        in_specs=in_specs,
        out_specs=P(("dp", "ctx"), "head"),
        check_vma=False,
    )
```

```python
import functools

import jax
import jax.numpy as jnp
from jax import lax
from jax.experimental import pallas as pl
from jax.experimental.pallas import tpu as pltpu
from jax.sharding import PartitionSpec as P

MESH = pl.DeviceIdType.MESH
HEAD_DIM = 256
NEG_FILL = -1e30
SCALE = HEAD_DIM ** (-0.5)
F32 = jnp.float32
BF16 = jnp.bfloat16


def nt(a, b):
    return lax.dot_general(a, b, (((1,), (1,)), ((), ())), preferred_element_type=F32)


def nn(a, b):
    return lax.dot_general(a, b, (((1,), (0,)), ((), ())), preferred_element_type=F32)


def column_of(row, count, step):
    n = row.shape[1]
    i = lax.broadcasted_iota(jnp.int32, (count, n), 0)
    j = lax.broadcasted_iota(jnp.int32, (count, n), 1)
    return jnp.sum(jnp.where(j == step * i, row, 0.0), axis=1, keepdims=True)


def kernel(
    sizes,
    q_hbm,
    k_hbm,
    v_hbm,
    docs_hbm,
    wk_hbm,
    wv_hbm,
    tq_hbm,
    out_ref,
    qv,
    kb,
    vb,
    docs,
    tq,
    w,
    enc,
    acc,
    part_out,
    part_in,
    stat_out,
    stat_in,
    local_sem,
    halo_s,
    halo_r,
    small_s,
    small_r,
    map_s,
    z_r,
    y_r,
    o_r,
    sib_r,
    x_s,
    x_r,
    part_s,
    part_r,
    stat_s,
    stat_r,
):
    n_dp, n_ctx, n_x = sizes
    n_z = n_ctx // 4
    dp = lax.axis_index("dp")
    ctx = lax.axis_index("ctx")
    x = lax.axis_index("head")
    core = lax.rem(ctx, 2)
    yl = lax.rem(ctx // 2, 2)
    z = ctx // 4
    sign = 1 - 2 * yl

    heads = k_hbm.shape[1] // HEAD_DIM
    rows = k_hbm.shape[0]
    tgts = tq_hbm.shape[0]
    crosses = wk_hbm.shape[1] // HEAD_DIM
    wrows = wk_hbm.shape[0]

    left = (dp, lax.rem(ctx + n_ctx - 1, n_ctx), x)
    right = (dp, lax.rem(ctx + 1, n_ctx), x)
    long_to = (dp, lax.rem(ctx + n_ctx - 4 * sign, n_ctx), x)
    short_to = (dp, lax.rem(ctx + n_ctx + 4 * sign, n_ctx), x)
    pair = (dp, ctx + 2 - 4 * yl, x)
    across = (lax.rem(dp + 2 * yl - 1 + n_dp, n_dp), ctx + 2 - 4 * yl, x)
    sib = (dp, ctx + 1 - 2 * core, x)
    xp = (dp, ctx, lax.rem(x + 1, n_x))
    xm = (dp, ctx, lax.rem(x + n_x - 1, n_x))

    def remote(src, dst, send, recv, device):
        return pltpu.make_async_remote_copy(
            src_ref=src, dst_ref=dst, send_sem=send, recv_sem=recv,
            device_id=device, device_id_type=MESH,
        )

    def settle(ref, sem):
        pltpu.make_async_copy(ref, ref, sem).wait()

    def settle_rows(count, sem):
        settle(w.at[0, pl.ds(0, count)], sem)

    barrier = pltpu.get_barrier_semaphore()
    partners = (left, right, long_to, short_to, pair, across, sib, xp, xm)
    for device in partners:
        pl.semaphore_signal(barrier, inc=1, device_id=device, device_id_type=MESH)

    def place(parity, e):
        return parity * n_z + (e + 3) % n_z

    def shard(parity, e):
        return pl.ds(pl.multiple_of(place(parity, e) * HEAD_DIM + core * wrows, wrows), wrows)

    own_w = []
    for n in range(crosses):
        cols = pl.ds(n * HEAD_DIM, HEAD_DIM)
        for kv, src in enumerate((wk_hbm, wv_hbm)):
            own_w.append(pltpu.make_async_copy(
                src.at[:, cols], w.at[n, shard(0, 0), pl.ds(kv * HEAD_DIM, HEAD_DIM)], local_sem.at[4]))
    copies = [
        pltpu.make_async_copy(docs_hbm, docs.at[1], local_sem.at[0]),
        pltpu.make_async_copy(q_hbm, qv, local_sem.at[1]),
        pltpu.make_async_copy(tq_hbm, tq.at[2], local_sem.at[2]),
    ]
    for h in range(heads):
        cols = pl.ds(h * HEAD_DIM, HEAD_DIM)
        copies.append(pltpu.make_async_copy(k_hbm.at[:, cols], kb.at[1, h], local_sem.at[3]))
        copies.append(pltpu.make_async_copy(v_hbm.at[:, cols], vb.at[1, h], local_sem.at[3]))
    for copy in own_w:
        copy.start()
    pl.semaphore_wait(barrier, len(partners))

    counts = {"map": 0, "sib": 0, "x": 0}

    def go(copy, kind=None):
        copy.start()
        if kind:
            counts[kind] += 1

    sides = ((left, 2), (right, 0))
    for side, (device, slot) in enumerate(sides):
        go(remote(docs_hbm, docs.at[slot], small_s.at[0], small_r.at[0], device))

    def start_halo(h):
        cols = pl.ds(h * HEAD_DIM, HEAD_DIM)
        for side, (device, slot) in enumerate(sides):
            go(remote(k_hbm.at[:, cols], kb.at[slot, h], halo_s.at[0], halo_r.at[h], device))
            go(remote(v_hbm.at[:, cols], vb.at[slot, h], halo_s.at[0], halo_r.at[h], device))

    far_y = ((4, 0), (5, 0))
    held_back = ((2, 1), (4, 0))
    by_ring = ((6, 0), (6, 1), (4, 1))
    last = (2, 3, 4)
    z_pieces = [(ring, step, n) for ring, far in ((0, 5), (1, 3)) for step in range(1, far + 1)
                for n in range(crosses) if step < far or n == ring]
    y_pieces = [(e, n) for e in range(n_z) for n in range(crosses) if ((n_z - e) % n_z, n) not in by_ring]
    o_pieces = [(0, 0), (0, 1), (1, 1)]

    def send_z(ring, step, n):
        e = step - 1 if ring == 0 else 1 - step
        there = step if ring == 0 else n_z - step
        src, dst = w.at[n, shard(0, e)], w.at[n, shard(0, there)]
        go(remote(
            src, dst, map_s.at[0], z_r.at[z_pieces.index((ring, step, n))],
            long_to if ring == 0 else short_to), "map")

    def send_y(e, n):
        if (e, n) in by_ring:
            return
        there = (n_z - e) % n_z
        src, dst = w.at[n, shard(0, e)], w.at[n, shard(1, there)]
        go(remote(
            src, dst, map_s.at[0], y_r.at[y_pieces.index((there, n))],
            pair if (e, n) in far_y else across), "map")

    def send_sib(parity, e, n):
        at = w.at[n, shard(parity, e)]
        group = 1 if parity == 1 and e in last else 0
        go(remote(at, at, map_s.at[1], sib_r.at[n, group], sib), "sib")

    def arrive(ring, step, n):
        settle_rows(wrows, z_r.at[z_pieces.index((ring, step, n))])
        e = step if ring == 0 else n_z - step
        if ring == 0 and (step < 4 or (step == 4 and n == 0)):
            send_z(0, step + 1, n)
        if ring == 1 and (step < 2 or (step == 2 and n == 1)):
            send_z(1, step + 1, n)
        if (e, n) not in held_back:
            send_y(e, n)
        send_sib(0, e, n)

    def send_o(ring, n):
        src = w.at[n, shard(1, 1 if ring == 0 else 5)]
        dst = w.at[n, shard(1, 2 if ring == 0 else 4)]
        go(remote(
            src, dst, map_s.at[0], o_r.at[o_pieces.index((ring, n))],
            long_to if ring == 0 else short_to), "map")

    def come_o(ring, n):
        settle_rows(wrows, o_r.at[o_pieces.index((ring, n))])
        send_sib(1, 2 if ring == 0 else 4, n)

    def come_y(e, n):
        settle_rows(wrows, y_r.at[y_pieces.index((e, n))])
        send_sib(1, e, n)

    start_halo(0)
    for copy in copies:
        copy.start()
    settle_rows(crosses * wrows, local_sem.at[4])
    for n in range(crosses):
        send_z(0, 1, n)
        send_z(1, 1, n)
        send_y(0, n)
    for h in range(1, heads):
        start_halo(h)
    for n in range(crosses):
        send_sib(0, 0, n)

    for copy in copies[:3]:
        copy.wait()
    settle_rows(2 * heads * rows // 2, local_sem.at[3])
    settle(docs.at[0:2], small_r.at[0])

    marks = [docs[slot].astype(F32) for slot in range(3)]
    own_col = column_of(marks[1], rows, 1)
    tgt_col = [column_of(marks[slot], tgts, rows // tgts) for slot in range(3)]
    side_col = jnp.concatenate([tgt_col[0], tgt_col[2]], axis=0)

    def enc_cols(at_x, h):
        e = lax.rem(sign * (at_x * 2 + h // 2 - z) + 2 * n_z + 3, n_z)
        parity = yl if h % 2 == 0 else 1 - yl
        return pl.ds(pl.multiple_of((parity * n_z + e) * HEAD_DIM, HEAD_DIM), HEAD_DIM)

    def half_rows(half):
        return pl.ds(half * (rows // 2), rows // 2)

    def attend(h):
        settle_rows(2 * rows, halo_r.at[h])
        query = qv[:, h * HEAD_DIM:(h + 1) * HEAD_DIM]
        scores = []
        for slot in range(3):
            raw = nt(query, kb[slot, h]) * SCALE
            scores.append(jnp.where(own_col == marks[slot], raw, NEG_FILL))
        top = jnp.max(jnp.maximum(jnp.maximum(scores[0], scores[1]), scores[2]), axis=1, keepdims=True)
        weights = [jnp.exp(s - top) for s in scores]
        total = jnp.sum(weights[0] + weights[1] + weights[2], axis=1, keepdims=True)
        summed = sum(nn(weights[slot].astype(BF16), vb[slot, h]) for slot in range(3))
        at = enc_cols(x, h)
        enc[:, at] = (summed / total).astype(BF16)
        for part in range(2):
            for side, device in enumerate((xp, xm)):
                piece = enc.at[half_rows(part if side == 0 else 1 - part), at]
                go(remote(piece, piece, x_s.at[0], x_r.at[h if part == 0 else heads], device), "x")

    def hand_on(h):
        settle_rows(rows // 2, x_r.at[h])
        for side, device in enumerate((xp, xm)):
            source = lax.rem(x + n_x - 1, n_x) if side == 0 else lax.rem(x + 1, n_x)
            at = enc_cols(source, h)
            piece = enc.at[half_rows(side), at]
            go(remote(piece, piece, x_s.at[0], x_r.at[heads], device), "x")

    def send_targets():
        for side in range(2):
            go(remote(tq_hbm, tq.at[1 - side], small_s.at[1], small_r.at[1], sides[side][0]))

    arrive(0, 1, 0)
    come_y(0, 0)
    arrive(0, 1, 1)
    attend(0)
    come_y(0, 1)
    arrive(1, 1, 0)
    arrive(0, 2, 0)
    come_y(7, 0)
    arrive(0, 2, 1)
    arrive(1, 1, 1)
    attend(1)
    hand_on(0)
    come_y(7, 1)
    arrive(0, 3, 0)
    arrive(0, 3, 1)
    send_y(2, 1)
    arrive(1, 2, 0)
    attend(2)
    hand_on(1)
    come_y(1, 0)
    come_y(6, 0)
    arrive(0, 4, 0)
    send_o(0, 0)
    arrive(0, 4, 1)
    arrive(1, 2, 1)
    send_y(4, 0)
    attend(3)
    send_targets()
    hand_on(2)
    come_y(1, 1)
    send_o(0, 1)
    arrive(0, 5, 0)
    come_y(5, 0)
    come_y(5, 1)
    send_o(1, 1)
    hand_on(3)
    arrive(1, 3, 1)
    come_y(4, 0)
    come_o(0, 0)
    come_y(6, 1)

    settle_rows(heads * rows, x_r.at[heads])

    split = (2 * n_z - len(last)) * HEAD_DIM

    def maps_most(n):
        settle_rows((2 * n_z - len(last)) * wrows, sib_r.at[n, 0])
        acc[n] = nn(enc[:, :split], w[n, :split])

    def maps_rest(n):
        settle_rows(len(last) * wrows, sib_r.at[n, 1])
        both = (acc[n] + nn(enc[:, split:], w[n, split:])).astype(BF16)
        return both[:, :HEAD_DIM], both[:, HEAD_DIM:]

    def partial_sums(query, col, memory):
        raw = nt(query, memory[0]) * SCALE
        scores = jnp.where(col == marks[1], raw, NEG_FILL)
        top = jnp.max(scores, axis=1, keepdims=True)
        weights = jnp.exp(scores - top)
        total = jnp.sum(weights, axis=1, keepdims=True)
        return top, total, nn(weights.astype(BF16), memory[1])

    diagonal = lax.broadcasted_iota(jnp.int32, (tgts, HEAD_DIM), 0) == lax.broadcasted_iota(
        jnp.int32, (tgts, HEAD_DIM), 1)
    first_row = lax.broadcasted_iota(jnp.int32, (8, HEAD_DIM), 0) == 0

    def row_of(column):
        return jnp.sum(jnp.where(diagonal, column, 0.0), axis=0, keepdims=True)

    def give(n, memory):
        query = tq[0:2, :, n * HEAD_DIM:(n + 1) * HEAD_DIM].reshape(2 * tgts, HEAD_DIM)
        top, total, summed = partial_sums(query, side_col, memory)
        for side in range(2):
            at = slice(side * tgts, (side + 1) * tgts)
            part_out[side, n] = summed[at].astype(BF16)
            stat_out[side, n] = jnp.where(first_row, row_of(top[at]), row_of(total[at]))
            go(remote(part_out.at[side, n], part_in.at[1 - side, n], part_s.at[0], part_r.at[n], sides[side][0]))
            go(remote(stat_out.at[side, n], stat_in.at[1 - side, n], stat_s.at[0], stat_r.at[n], sides[side][0]))

    def merge(n, own):
        settle(stat_in.at[:, n], stat_r.at[n])
        settle(part_in.at[:, n], part_r.at[n])
        tops, totals, sums = [own[0]], [own[1]], [own[2]]
        for side in range(2):
            tops.append(column_of(stat_in[1 - side, n, 0:1], tgts, 1))
            totals.append(column_of(stat_in[1 - side, n, 1:2], tgts, 1))
            sums.append(part_in[1 - side, n].astype(F32))
        most = jnp.maximum(jnp.maximum(tops[0], tops[1]), tops[2])
        factor = [jnp.exp(t - most) for t in tops]
        total = sum(f * t for f, t in zip(factor, totals))
        summed = sum(f * s for f, s in zip(factor, sums))
        out_ref[:, n * HEAD_DIM:(n + 1) * HEAD_DIM] = summed / total

    settle(tq.at[0:2], small_r.at[1])
    maps_most(0)
    come_y(3, 0)
    come_o(0, 1)
    come_o(1, 1)
    come_y(3, 1)
    maps_most(1)
    memory = {}
    for n in range(crosses):
        memory[n] = maps_rest(n)
        give(n, memory[n])
    own = [
        partial_sums(tq[2, :, n * HEAD_DIM:(n + 1) * HEAD_DIM], tgt_col[1], memory[n]) for n in range(crosses)
    ]
    for n in range(crosses):
        merge(n, own[n])

    settle(docs.at[0:2], small_s.at[0])
    settle(tq.at[0:2], small_s.at[1])
    settle(part_out, part_s.at[0])
    settle(stat_out, stat_s.at[0])
    settle_rows(2 * heads * rows, halo_s.at[0])
    settle_rows(counts["x"] * rows // 4, x_s.at[0])
    settle_rows(counts["map"] * wrows, map_s.at[0])
    settle_rows(counts["sib"] * wrows, map_s.at[1])


def on_device(sizes, enc_query, enc_key, enc_value, doc_ids, key_map, value_map, tgt_query):
    rows, width = enc_key.shape
    heads = width // HEAD_DIM
    wrows, wcols = key_map.shape
    crosses = wcols // HEAD_DIM
    tgts = tgt_query.shape[0]
    n_z = sizes[1] // 4
    docs = doc_ids.reshape(1, rows)
    dma = pltpu.SemaphoreType.DMA
    any_spec = pl.BlockSpec(memory_space=pl.ANY)
    out = pl.pallas_call(
        functools.partial(kernel, sizes),
        out_shape=pltpu.VMEM((tgts, wcols), F32),
        in_specs=[any_spec] * 7,
        out_specs=pl.BlockSpec(memory_space=pltpu.VMEM),
        scratch_shapes=[
            pltpu.VMEM((rows, width), BF16),
            pltpu.VMEM((3, heads, rows, HEAD_DIM), BF16),
            pltpu.VMEM((3, heads, rows, HEAD_DIM), BF16),
            pltpu.VMEM((3, 1, rows), jnp.int32),
            pltpu.VMEM((3, tgts, wcols), BF16),
            pltpu.VMEM((crosses, wrows * sizes[1], 2 * HEAD_DIM), BF16),
            pltpu.VMEM((rows, width * sizes[2]), BF16),
            pltpu.VMEM((crosses, rows, 2 * HEAD_DIM), F32),
            pltpu.VMEM((2, crosses, tgts, HEAD_DIM), BF16),
            pltpu.VMEM((2, crosses, tgts, HEAD_DIM), BF16),
            pltpu.VMEM((2, crosses, 8, HEAD_DIM), F32),
            pltpu.VMEM((2, crosses, 8, HEAD_DIM), F32),
            dma((5,)),
            dma((1,)),
            dma((heads,)),
            dma((2,)),
            dma((2,)),
            dma((2,)),
            dma((14,)),
            dma((13,)),
            dma((3,)),
            dma((crosses, 2)),
            dma((1,)),
            dma((heads + 1,)),
            dma((1,)),
            dma((crosses,)),
            dma((1,)),
            dma((crosses,)),
        ],
        compiler_params=pltpu.CompilerParams(
            collective_id=0, has_side_effects=True, vmem_limit_bytes=60 * 1024 * 1024
        ),
    )(enc_query, enc_key, enc_value, docs, key_map, value_map, tgt_query)
    return out.astype(BF16)


def solution(mesh):
    sizes = (mesh.shape["dp"], mesh.shape["ctx"], mesh.shape["head"])
    in_specs = (
        P(("dp", "ctx"), "head"),
        P(("dp", "ctx"), "head"),
        P(("dp", "ctx"), "head"),
        P(("dp", "ctx")),
        P("ctx", "head"),
        P("ctx", "head"),
        P(("dp", "ctx"), "head"),
    )
    return jax.shard_map(
        functools.partial(on_device, sizes),
        mesh=mesh,
        in_specs=in_specs,
        out_specs=P(("dp", "ctx"), "head"),
        check_vma=False,
    )
```

```python
import functools

import jax
import jax.numpy as jnp
from jax import lax
from jax.experimental import pallas as pl
from jax.experimental.pallas import tpu as pltpu
from jax.sharding import PartitionSpec as P

MESH = pl.DeviceIdType.MESH
HEAD_DIM = 256
NEG_FILL = -1e30
SCALE = HEAD_DIM ** (-0.5)
F32 = jnp.float32
BF16 = jnp.bfloat16


def nt(a, b):
    return lax.dot_general(a, b, (((1,), (1,)), ((), ())), preferred_element_type=F32)


def nn(a, b):
    return lax.dot_general(a, b, (((1,), (0,)), ((), ())), preferred_element_type=F32)


def column_of(row, count, step):
    n = row.shape[1]
    i = lax.broadcasted_iota(jnp.int32, (count, n), 0)
    j = lax.broadcasted_iota(jnp.int32, (count, n), 1)
    return jnp.sum(jnp.where(j == step * i, row, 0.0), axis=1, keepdims=True)


def kernel(
    sizes,
    q_hbm,
    k_hbm,
    v_hbm,
    docs_hbm,
    wk_hbm,
    wv_hbm,
    tq_hbm,
    out_ref,
    qv,
    kb,
    vb,
    docs,
    tq,
    w,
    enc,
    acc,
    part_out,
    part_in,
    stat_out,
    stat_in,
    local_sem,
    halo_s,
    halo_r,
    small_s,
    small_r,
    map_s,
    z_r,
    y_r,
    o_r,
    sib_r,
    x_s,
    x_r,
    part_s,
    part_r,
    stat_s,
    stat_r,
):
    n_dp, n_ctx, n_x = sizes
    n_z = n_ctx // 4
    dp = lax.axis_index("dp")
    ctx = lax.axis_index("ctx")
    x = lax.axis_index("head")
    core = lax.rem(ctx, 2)
    yl = lax.rem(ctx // 2, 2)
    z = ctx // 4
    sign = 1 - 2 * yl

    heads = k_hbm.shape[1] // HEAD_DIM
    rows = k_hbm.shape[0]
    tgts = tq_hbm.shape[0]
    crosses = wk_hbm.shape[1] // HEAD_DIM
    wrows = wk_hbm.shape[0]

    left = (dp, lax.rem(ctx + n_ctx - 1, n_ctx), x)
    right = (dp, lax.rem(ctx + 1, n_ctx), x)
    long_to = (dp, lax.rem(ctx + n_ctx - 4 * sign, n_ctx), x)
    short_to = (dp, lax.rem(ctx + n_ctx + 4 * sign, n_ctx), x)
    pair = (dp, ctx + 2 - 4 * yl, x)
    across = (lax.rem(dp + 2 * yl - 1 + n_dp, n_dp), ctx + 2 - 4 * yl, x)
    sib = (dp, ctx + 1 - 2 * core, x)
    xp = (dp, ctx, lax.rem(x + 1, n_x))
    xm = (dp, ctx, lax.rem(x + n_x - 1, n_x))

    def remote(src, dst, send, recv, device):
        return pltpu.make_async_remote_copy(
            src_ref=src, dst_ref=dst, send_sem=send, recv_sem=recv,
            device_id=device, device_id_type=MESH,
        )

    def settle(ref, sem):
        pltpu.make_async_copy(ref, ref, sem).wait()

    def settle_rows(count, sem):
        settle(w.at[0, pl.ds(0, count)], sem)

    barrier = pltpu.get_barrier_semaphore()
    partners = (left, right, long_to, short_to, pair, across, sib, xp, xm)
    for device in partners:
        pl.semaphore_signal(barrier, inc=1, device_id=device, device_id_type=MESH)

    def place(parity, e):
        return parity * n_z + (e + 3) % n_z

    def shard(parity, e):
        return pl.ds(pl.multiple_of(place(parity, e) * HEAD_DIM + core * wrows, wrows), wrows)

    own_w = []
    for n in range(crosses):
        cols = pl.ds(n * HEAD_DIM, HEAD_DIM)
        for kv, src in enumerate((wk_hbm, wv_hbm)):
            own_w.append(pltpu.make_async_copy(
                src.at[:, cols], w.at[n, shard(0, 0), pl.ds(kv * HEAD_DIM, HEAD_DIM)], local_sem.at[4]))
    copies = [
        pltpu.make_async_copy(docs_hbm, docs.at[1], local_sem.at[0]),
        pltpu.make_async_copy(q_hbm, qv, local_sem.at[1]),
        pltpu.make_async_copy(tq_hbm, tq.at[2], local_sem.at[2]),
    ]
    for h in range(heads):
        cols = pl.ds(h * HEAD_DIM, HEAD_DIM)
        copies.append(pltpu.make_async_copy(k_hbm.at[:, cols], kb.at[1, h], local_sem.at[3]))
        copies.append(pltpu.make_async_copy(v_hbm.at[:, cols], vb.at[1, h], local_sem.at[3]))
    for copy in own_w:
        copy.start()
    pl.semaphore_wait(barrier, len(partners))

    counts = {"map": 0, "sib": 0}

    def go(copy, kind=None):
        copy.start()
        if kind:
            counts[kind] += 1

    sides = ((left, 2), (right, 0))
    for side, (device, slot) in enumerate(sides):
        go(remote(docs_hbm, docs.at[slot], small_s.at[0], small_r.at[0], device))

    def start_halo(h):
        cols = pl.ds(h * HEAD_DIM, HEAD_DIM)
        for side, (device, slot) in enumerate(sides):
            go(remote(k_hbm.at[:, cols], kb.at[slot, h], halo_s.at[0], halo_r.at[h], device))
            go(remote(v_hbm.at[:, cols], vb.at[slot, h], halo_s.at[0], halo_r.at[h], device))

    far_y = ((4, 0), (5, 0))
    held_back = ((2, 1), (4, 0))
    by_ring = ((6, 0), (6, 1), (4, 1))
    last = (2, 3, 4)
    z_pieces = [(ring, step, n) for ring, far in ((0, 5), (1, 3)) for step in range(1, far + 1)
                for n in range(crosses) if step < far or n == ring]
    y_pieces = [(e, n) for e in range(n_z) for n in range(crosses) if ((n_z - e) % n_z, n) not in by_ring]
    o_pieces = [(0, 0), (0, 1), (1, 1)]

    def send_z(ring, step, n):
        e = step - 1 if ring == 0 else 1 - step
        there = step if ring == 0 else n_z - step
        src, dst = w.at[n, shard(0, e)], w.at[n, shard(0, there)]
        go(remote(
            src, dst, map_s.at[0], z_r.at[z_pieces.index((ring, step, n))],
            long_to if ring == 0 else short_to), "map")

    def send_y(e, n):
        if (e, n) in by_ring:
            return
        there = (n_z - e) % n_z
        src, dst = w.at[n, shard(0, e)], w.at[n, shard(1, there)]
        go(remote(
            src, dst, map_s.at[0], y_r.at[y_pieces.index((there, n))],
            pair if (e, n) in far_y else across), "map")

    def send_sib(parity, e, n):
        at = w.at[n, shard(parity, e)]
        group = 1 if parity == 1 and e in last else 0
        go(remote(at, at, map_s.at[1], sib_r.at[n, group], sib), "sib")

    def arrive(ring, step, n):
        settle_rows(wrows, z_r.at[z_pieces.index((ring, step, n))])
        e = step if ring == 0 else n_z - step
        if ring == 0 and (step < 4 or (step == 4 and n == 0)):
            send_z(0, step + 1, n)
        if ring == 1 and (step < 2 or (step == 2 and n == 1)):
            send_z(1, step + 1, n)
        if (e, n) not in held_back:
            send_y(e, n)
        send_sib(0, e, n)

    def send_o(ring, n):
        src = w.at[n, shard(1, 1 if ring == 0 else 5)]
        dst = w.at[n, shard(1, 2 if ring == 0 else 4)]
        go(remote(
            src, dst, map_s.at[0], o_r.at[o_pieces.index((ring, n))],
            long_to if ring == 0 else short_to), "map")

    def come_o(ring, n):
        settle_rows(wrows, o_r.at[o_pieces.index((ring, n))])
        send_sib(1, 2 if ring == 0 else 4, n)

    def come_y(e, n):
        settle_rows(wrows, y_r.at[y_pieces.index((e, n))])
        send_sib(1, e, n)

    start_halo(0)
    for copy in copies:
        copy.start()
    settle_rows(crosses * wrows, local_sem.at[4])
    for n in range(crosses):
        send_z(0, 1, n)
        send_z(1, 1, n)
        send_y(0, n)
    for h in range(1, heads):
        start_halo(h)
    for n in range(crosses):
        send_sib(0, 0, n)

    for copy in copies[:3]:
        copy.wait()
    settle_rows(2 * heads * rows // 2, local_sem.at[3])
    settle(docs.at[0:2], small_r.at[0])

    marks = [docs[slot].astype(F32) for slot in range(3)]
    own_col = column_of(marks[1], rows, 1)
    tgt_col = [column_of(marks[slot], tgts, rows // tgts) for slot in range(3)]
    side_col = jnp.concatenate([tgt_col[0], tgt_col[2]], axis=0)

    def enc_cols(at_x, h):
        e = lax.rem(sign * (at_x * 2 + h // 2 - z) + 2 * n_z + 3, n_z)
        parity = yl if h % 2 == 0 else 1 - yl
        return pl.ds(pl.multiple_of((parity * n_z + e) * HEAD_DIM, HEAD_DIM), HEAD_DIM)

    half, quarter = rows // 2, rows // 4
    pieces = (
        (pl.ds(0, quarter), pl.ds(quarter, quarter), pl.ds(half, half)),
        (pl.ds(half, quarter), pl.ds(half + quarter, quarter), pl.ds(0, half)),
    )

    def attend(h):
        settle_rows(2 * rows, halo_r.at[h])
        query = qv[:, h * HEAD_DIM:(h + 1) * HEAD_DIM]
        scores = []
        for slot in range(3):
            raw = nt(query, kb[slot, h]) * SCALE
            scores.append(jnp.where(own_col == marks[slot], raw, NEG_FILL))
        top = jnp.max(jnp.maximum(jnp.maximum(scores[0], scores[1]), scores[2]), axis=1, keepdims=True)
        weights = [jnp.exp(s - top) for s in scores]
        total = jnp.sum(weights[0] + weights[1] + weights[2], axis=1, keepdims=True)
        summed = sum(nn(weights[slot].astype(BF16), vb[slot, h]) for slot in range(3))
        at = enc_cols(x, h)
        enc[:, at] = (summed / total).astype(BF16)
        for part in range(3):
            for side, device in enumerate((xp, xm)):
                piece = enc.at[pieces[side][part], at]
                go(remote(piece, piece, x_s.at[0], x_r.at[2 * h + part if part < 2 else 2 * heads], device))

    def hand_on(h):
        for part in range(2):
            settle_rows(quarter, x_r.at[2 * h + part])
            for side, device in enumerate((xp, xm)):
                source = lax.rem(x + n_x - 1, n_x) if side == 0 else lax.rem(x + 1, n_x)
                piece = enc.at[pieces[side][part], enc_cols(source, h)]
                go(remote(piece, piece, x_s.at[0], x_r.at[2 * heads], device))

    def send_targets():
        for side in range(2):
            go(remote(tq_hbm, tq.at[1 - side], small_s.at[1], small_r.at[1], sides[side][0]))

    arrive(0, 1, 0)
    come_y(0, 0)
    arrive(0, 1, 1)
    attend(0)
    come_y(0, 1)
    arrive(1, 1, 0)
    arrive(0, 2, 0)
    come_y(7, 0)
    arrive(0, 2, 1)
    arrive(1, 1, 1)
    attend(1)
    hand_on(0)
    come_y(7, 1)
    arrive(0, 3, 0)
    arrive(0, 3, 1)
    send_y(2, 1)
    arrive(1, 2, 0)
    attend(2)
    hand_on(1)
    come_y(1, 0)
    come_y(6, 0)
    arrive(0, 4, 0)
    send_o(0, 0)
    arrive(0, 4, 1)
    arrive(1, 2, 1)
    send_y(4, 0)
    attend(3)
    send_targets()
    hand_on(2)
    come_y(1, 1)
    send_o(0, 1)
    arrive(0, 5, 0)
    come_y(5, 0)
    come_y(5, 1)
    send_o(1, 1)
    hand_on(3)
    arrive(1, 3, 1)
    come_y(4, 0)
    come_o(0, 0)
    come_y(6, 1)
    come_o(0, 1)
    come_y(3, 0)

    settle_rows(heads * rows, x_r.at[2 * heads])

    split = (2 * n_z - len(last)) * HEAD_DIM

    def maps_most(n):
        settle_rows((2 * n_z - len(last)) * wrows, sib_r.at[n, 0])
        acc[n] = nn(enc[:, :split], w[n, :split])

    def maps_rest(n):
        settle_rows(len(last) * wrows, sib_r.at[n, 1])
        both = (acc[n] + nn(enc[:, split:], w[n, split:])).astype(BF16)
        return both[:, :HEAD_DIM], both[:, HEAD_DIM:]

    def partial_sums(query, col, memory):
        raw = nt(query, memory[0]) * SCALE
        scores = jnp.where(col == marks[1], raw, NEG_FILL)
        top = jnp.max(scores, axis=1, keepdims=True)
        weights = jnp.exp(scores - top)
        total = jnp.sum(weights, axis=1, keepdims=True)
        return top, total, nn(weights.astype(BF16), memory[1])

    diagonal = lax.broadcasted_iota(jnp.int32, (tgts, HEAD_DIM), 0) == lax.broadcasted_iota(
        jnp.int32, (tgts, HEAD_DIM), 1)
    first_row = lax.broadcasted_iota(jnp.int32, (8, HEAD_DIM), 0) == 0

    def row_of(column):
        return jnp.sum(jnp.where(diagonal, column, 0.0), axis=0, keepdims=True)

    def give(n, memory):
        query = tq[0:2, :, n * HEAD_DIM:(n + 1) * HEAD_DIM].reshape(2 * tgts, HEAD_DIM)
        top, total, summed = partial_sums(query, side_col, memory)
        for side in range(2):
            at = slice(side * tgts, (side + 1) * tgts)
            part_out[side, n] = summed[at].astype(BF16)
            stat_out[side, n] = jnp.where(first_row, row_of(top[at]), row_of(total[at]))
            go(remote(part_out.at[side, n], part_in.at[1 - side, n], part_s.at[0], part_r.at[n], sides[side][0]))
            go(remote(stat_out.at[side, n], stat_in.at[1 - side, n], stat_s.at[0], stat_r.at[n], sides[side][0]))

    def merge(n, own):
        settle(stat_in.at[:, n], stat_r.at[n])
        settle(part_in.at[:, n], part_r.at[n])
        tops, totals, sums = [own[0]], [own[1]], [own[2]]
        for side in range(2):
            tops.append(column_of(stat_in[1 - side, n, 0:1], tgts, 1))
            totals.append(column_of(stat_in[1 - side, n, 1:2], tgts, 1))
            sums.append(part_in[1 - side, n].astype(F32))
        most = jnp.maximum(jnp.maximum(tops[0], tops[1]), tops[2])
        factor = [jnp.exp(t - most) for t in tops]
        total = sum(f * t for f, t in zip(factor, totals))
        summed = sum(f * s for f, s in zip(factor, sums))
        out_ref[:, n * HEAD_DIM:(n + 1) * HEAD_DIM] = summed / total

    settle(tq.at[0:2], small_r.at[1])
    maps_most(0)
    come_o(1, 1)
    maps_most(1)
    come_y(3, 1)
    memory = {}
    for n in range(crosses):
        memory[n] = maps_rest(n)
        give(n, memory[n])
    own = [
        partial_sums(tq[2, :, n * HEAD_DIM:(n + 1) * HEAD_DIM], tgt_col[1], memory[n]) for n in range(crosses)
    ]
    for n in range(crosses):
        merge(n, own[n])

    settle(docs.at[0:2], small_s.at[0])
    settle(tq.at[0:2], small_s.at[1])
    settle(part_out, part_s.at[0])
    settle(stat_out, stat_s.at[0])
    settle_rows(2 * heads * rows, halo_s.at[0])
    settle_rows(3 * heads * rows // 2, x_s.at[0])
    settle_rows(counts["map"] * wrows, map_s.at[0])
    settle_rows(counts["sib"] * wrows, map_s.at[1])


def on_device(sizes, enc_query, enc_key, enc_value, doc_ids, key_map, value_map, tgt_query):
    rows, width = enc_key.shape
    heads = width // HEAD_DIM
    wrows, wcols = key_map.shape
    crosses = wcols // HEAD_DIM
    tgts = tgt_query.shape[0]
    n_z = sizes[1] // 4
    docs = doc_ids.reshape(1, rows)
    dma = pltpu.SemaphoreType.DMA
    any_spec = pl.BlockSpec(memory_space=pl.ANY)
    out = pl.pallas_call(
        functools.partial(kernel, sizes),
        out_shape=pltpu.VMEM((tgts, wcols), F32),
        in_specs=[any_spec] * 7,
        out_specs=pl.BlockSpec(memory_space=pltpu.VMEM),
        scratch_shapes=[
            pltpu.VMEM((rows, width), BF16),
            pltpu.VMEM((3, heads, rows, HEAD_DIM), BF16),
            pltpu.VMEM((3, heads, rows, HEAD_DIM), BF16),
            pltpu.VMEM((3, 1, rows), jnp.int32),
            pltpu.VMEM((3, tgts, wcols), BF16),
            pltpu.VMEM((crosses, wrows * sizes[1], 2 * HEAD_DIM), BF16),
            pltpu.VMEM((rows, width * sizes[2]), BF16),
            pltpu.VMEM((crosses, rows, 2 * HEAD_DIM), F32),
            pltpu.VMEM((2, crosses, tgts, HEAD_DIM), BF16),
            pltpu.VMEM((2, crosses, tgts, HEAD_DIM), BF16),
            pltpu.VMEM((2, crosses, 8, HEAD_DIM), F32),
            pltpu.VMEM((2, crosses, 8, HEAD_DIM), F32),
            dma((5,)),
            dma((1,)),
            dma((heads,)),
            dma((2,)),
            dma((2,)),
            dma((2,)),
            dma((14,)),
            dma((13,)),
            dma((3,)),
            dma((crosses, 2)),
            dma((1,)),
            dma((2 * heads + 1,)),
            dma((1,)),
            dma((crosses,)),
            dma((1,)),
            dma((crosses,)),
        ],
        compiler_params=pltpu.CompilerParams(
            collective_id=0, has_side_effects=True, vmem_limit_bytes=60 * 1024 * 1024
        ),
    )(enc_query, enc_key, enc_value, docs, key_map, value_map, tgt_query)
    return out.astype(BF16)


def solution(mesh):
    sizes = (mesh.shape["dp"], mesh.shape["ctx"], mesh.shape["head"])
    in_specs = (
        P(("dp", "ctx"), "head"),
        P(("dp", "ctx"), "head"),
        P(("dp", "ctx"), "head"),
        P(("dp", "ctx")),
        P("ctx", "head"),
        P("ctx", "head"),
        P(("dp", "ctx"), "head"),
    )
    return jax.shard_map(
        functools.partial(on_device, sizes),
        mesh=mesh,
        in_specs=in_specs,
        out_specs=P(("dp", "ctx"), "head"),
        check_vma=False,
    )
```
